256 devices in a mesh: seq: 4 (over x_lo, core), dp: 64 (over x_hi, y, z).
Axes of the slice: x: 4 (x_hi: 2, x_lo: 2; x = x_hi * 2 + x_lo), y: 4, z: 8, core: 2. Of those that a mesh axis runs over, the one named last changes fastest.
Arguments:
- residual: bfloat16 [49152, 2560], P(('seq', 'dp')), may hold values from -6 to 6
- query_raw: bfloat16 [49152, 2560], P(('seq', 'dp')), may hold values from -60 to 60
- key_raw: bfloat16 [49152, 2560], P(('seq', 'dp')), may hold values from -60 to 60
- values: bfloat16 [49152, 2560], P(('seq', 'dp')), may hold values from -6 to 6
- residual_grad: bfloat16 [49152, 2560], P(('seq', 'dp')), may hold values from -6 to 6
- modulated_grad: bfloat16 [49152, 2560], P(('seq', 'dp')), may hold values from -24 to 24
- condition: float32 [64, 2, 2560], P('dp'), may hold values from -3 to 3
- modulation: float32 [2, 2560], P(None, ('seq', 'dp')), may hold values from -0.5 to 0.5
- norm_gains: float32 [2, 2560], P(None, ('seq', 'dp')), may hold values from 0.25 to 1.75
Outputs:
- input_grad: bfloat16 [49152, 2560], P(('seq', 'dp'))
- query_grad: bfloat16 [49152, 2560], P(('seq', 'dp'))
- key_grad: bfloat16 [49152, 2560], P(('seq', 'dp'))
- value_grad: bfloat16 [49152, 2560], P(('seq', 'dp'))
- param_grads: float32 [5, 2560], P(None, ('seq', 'dp'))
The draws below stay inside these ranges and needn't reach their ends.
All inputs are finite; a program needn't handle non-finite values.
Results may differ from the reference program's by a relative error of at most 0.009.
The reference program's roundings to bfloat16 on the way (of `normed_query`, `normed_key`, `weights_low`, `attended`, `attended_grad` and `score_grad`) count: a program that leaves them out, or rounds other values in their place, can miss the bound.
Values may be sent and summed in bfloat16 or wider, within the bound.
A program may use at most 128 MiB of HBM per device.

```python
import jax
import jax.numpy as jnp
from jax import lax

HEAD_DIM = 128
D = 2560
TOK_DEV = 192
TOKENS = 768
CLIPS = 64
ROWS = 49152
N_SEQ = 4
N_DP = 64


def query_key_pair(key):
    base_key = jax.random.fold_in(key, 7)
    subkeys = jax.random.split(base_key, 3)
    query = jnp.clip(jax.random.normal(subkeys[1], (ROWS, D)), -6.0, 6.0)
    keyrows = jnp.clip(jax.random.normal(subkeys[2], (ROWS, D)), -6.0, 6.0)
    return (query, keyrows)


def draw_query_raw(key, part):
    return query_key_pair(key)[0].astype(jnp.bfloat16)


def draw_key_raw(key, part):
    return query_key_pair(key)[1].astype(jnp.bfloat16)


def strengthened(result, own_key, source, target, shards_of, factor):
    owner, partner = [(jnp.arange(result.shape[dim]) // (result.shape[dim] // shards_of)).reshape([-1 if axis == dim else 1 for axis in range(result.ndim)]) for dim in (source, target)]
    chosen = jax.random.permutation(own_key, shards_of)[partner]
    strong = (owner == chosen) | (owner == (partner + shards_of // 2) % shards_of)
    return jnp.where(strong, factor * result, result)


def level_of(key, dims, shards, low, high):
    level, own = 1.0, jax.random.fold_in(key, 6)
    for dim, blocks in shards:
        draws = jnp.exp(jax.random.uniform(jax.random.fold_in(own, dim), (blocks,), jnp.float32, low / len(shards), high / len(shards)))
        level = level * jnp.repeat(draws, dims[dim] // blocks).reshape([-1 if axis == dim else 1 for axis in range(len(dims))])
    return level


def bell_draw(own_key, shape, scale, bound, cuts=(), kind=jnp.bfloat16):
    gain = level_of(own_key, shape, cuts, -0.22, 0.18) if cuts else 1.0
    drawn = jax.random.normal(own_key, shape, jnp.float32) * scale * gain
    return jnp.minimum(jnp.maximum(drawn, -bound), bound).astype(kind)


def noise_with(own_key, shape, deviation, reach, cuts, heavy, held_as=jnp.bfloat16):
    result = deviation * jax.random.normal(own_key, shape, jnp.float32)
    if cuts:
        result = result * level_of(own_key, shape, cuts, -0.22, 0.18)
    return jnp.clip(strengthened(result, jax.random.fold_in(own_key, 3), *heavy), -reach, reach).astype(held_as)


def setup_inputs(seed: int = 0) -> dict:
    keys = jax.random.split(jax.random.key(seed), 10)
    return {
        "residual": bell_draw(keys[0], (ROWS, D), 1.0, 6.0, ((0, 256),)),
        "query_raw": draw_query_raw(jax.random.fold_in(keys[9], 71), 0),
        "key_raw": draw_key_raw(jax.random.fold_in(keys[9], 71), 0),
        "values": bell_draw(keys[3], (ROWS, D), 1.0, 6.0, ((0, 256),)),
        "residual_grad": bell_draw(keys[4], (ROWS, D), 1.0, 6.0, ((0, 256),)),
        "modulated_grad": noise_with(keys[5], (ROWS, D), 1.0, 24.0, ((0, 256),), (0, 1, 256, 6.0)),
        "condition": bell_draw(keys[6], (CLIPS, 2, D), 0.5, 3.0, ((0, 64),), jnp.float32),
        "modulation": jnp.clip(jax.random.uniform(keys[7], (2, D), jnp.float32, -0.5, 0.5) * level_of(keys[7], (2, D), ((1, 256),), -0.4, 0.0), -0.5, 0.5),
        "norm_gains": jnp.clip(1.0 + 0.15 * jax.random.normal(keys[8], (2, D), jnp.float32), 0.25, 1.75),
    }


epsilon = 1e-06

def split_heads(matrix, head_width):
    row_count = matrix.shape[0]
    return matrix.reshape(row_count, -1, head_width).transpose(1, 0, 2)

def merge_heads(stacked):
    return stacked.transpose(1, 0, 2).reshape(stacked.shape[1], -1)

def root_scale(raw_values):
    floats = raw_values.astype(jnp.float32)
    return lax.rsqrt(lax.optimization_barrier(jnp.mean(floats * floats, axis=1, keepdims=True)) + epsilon)

def head_scores(query_head, key_head):
    return lax.dot_general(query_head, key_head, (((1,), (1,)), ((), ())), preferred_element_type=jnp.float32) * query_head.shape[-1] ** (-0.5)

def head_forward(pieces):
    query_head, key_head, value_head = pieces
    scores = head_scores(query_head, key_head)
    row_max = lax.optimization_barrier(jnp.max(scores, axis=1, keepdims=True))
    row_sum = lax.optimization_barrier(jnp.sum(jnp.exp(scores - row_max), axis=1, keepdims=True))
    logsum = row_max + jnp.log(row_sum)
    weights_low = jnp.exp(scores - logsum).astype(jnp.bfloat16)
    attended = jnp.dot(weights_low, value_head, preferred_element_type=jnp.float32).astype(jnp.bfloat16)
    return (attended, logsum[:, 0])

def head_backward(pieces):
    query_head, key_head, value_head, attended, attended_grad, logsum = pieces
    scores = head_scores(query_head, key_head)
    weights = jnp.exp(scores - logsum[:, None])
    row_dot = lax.optimization_barrier(jnp.sum(attended_grad.astype(jnp.float32) * attended.astype(jnp.float32), axis=1, keepdims=True))
    weight_grad = lax.dot_general(attended_grad, value_head, (((1,), (1,)), ((), ())), preferred_element_type=jnp.float32)
    score_grad = (weights * (weight_grad - row_dot) * query_head.shape[-1] ** (-0.5)).astype(jnp.bfloat16)
    value_part = lax.dot_general(weights.astype(jnp.bfloat16), attended_grad, (((0,), (0,)), ((), ())), preferred_element_type=jnp.float32)
    query_part = jnp.dot(score_grad, key_head, preferred_element_type=jnp.float32)
    key_part = lax.dot_general(score_grad, query_head, (((0,), (0,)), ((), ())), preferred_element_type=jnp.float32)
    return (query_part, key_part, value_part)

def stream_pass(residual, attended, modulated, residual_grad, modulated_grad):
    gate_row = modulated[0]
    scale_row = modulated[1]
    summed = residual.astype(jnp.float32) + gate_row * attended.astype(jnp.float32)
    centered = summed - lax.optimization_barrier(jnp.mean(summed, axis=1, keepdims=True))
    norm_scale = lax.rsqrt(lax.optimization_barrier(jnp.mean(centered * centered, axis=1, keepdims=True)) + epsilon)
    normed = centered * norm_scale
    scaled_grad = modulated_grad.astype(jnp.float32) * (1.0 + scale_row)
    stream_grad = residual_grad.astype(jnp.float32) + norm_scale * (scaled_grad - lax.optimization_barrier(jnp.mean(scaled_grad, axis=1, keepdims=True)) - normed * lax.optimization_barrier(jnp.mean(scaled_grad * normed, axis=1, keepdims=True)))
    attended_grad = (stream_grad * gate_row).astype(jnp.bfloat16)
    return (stream_grad, normed, attended_grad)

def norm_backward(raw_values, inverse, gain_row, upstream):
    floats = raw_values.astype(jnp.float32)
    weighted = gain_row * upstream
    return (inverse * weighted - floats * inverse ** 3 * lax.optimization_barrier(jnp.mean(floats * weighted, axis=1, keepdims=True))).astype(jnp.bfloat16)

def partial_sums(attended, stream_grad, normed, modulated_grad, query_raw, query_scale, query_part, key_raw, key_scale, key_part):
    grad_floats = modulated_grad.astype(jnp.float32)
    return jnp.stack([lax.optimization_barrier(jnp.sum(stream_grad * attended.astype(jnp.float32), axis=0)), lax.optimization_barrier(jnp.sum(grad_floats, axis=0)), lax.optimization_barrier(jnp.sum(grad_floats * normed, axis=0)), lax.optimization_barrier(jnp.sum(query_part * query_raw.astype(jnp.float32) * query_scale, axis=0)), lax.optimization_barrier(jnp.sum(key_part * key_raw.astype(jnp.float32) * key_scale, axis=0))])

def reference(residual, query_raw, key_raw, values, residual_grad, modulated_grad, condition, modulation, norm_gains):

    def clip_major(matrix):
        return matrix.reshape(N_SEQ, N_DP, TOK_DEV, D).transpose(1, 0, 2, 3).reshape(N_DP, TOKENS, D)

    def row_major(matrix):
        return matrix.reshape(N_DP, N_SEQ, TOK_DEV, D).transpose(1, 0, 2, 3).reshape(ROWS, D)

    def clip_pass(pieces):
        clip_resid, clip_query, clip_key, clip_values, clip_rgrad, clip_mgrad, clip_cond = pieces
        modulated = modulation + clip_cond
        query_scale = root_scale(clip_query)
        key_scale = root_scale(clip_key)
        normed_query = (clip_query.astype(jnp.float32) * query_scale * norm_gains[0]).astype(jnp.bfloat16)
        normed_key = (clip_key.astype(jnp.float32) * key_scale * norm_gains[1]).astype(jnp.bfloat16)
        query_heads = split_heads(normed_query, HEAD_DIM)
        key_heads = split_heads(normed_key, HEAD_DIM)
        value_heads = split_heads(clip_values, HEAD_DIM)
        attended_heads, logsum = lax.map(head_forward, (query_heads, key_heads, value_heads))
        attended = merge_heads(attended_heads)
        stream_grad, normed, attended_grad = stream_pass(clip_resid, attended, modulated, clip_rgrad, clip_mgrad)
        query_part, key_part, value_part = lax.map(head_backward, (query_heads, key_heads, value_heads, attended_heads, split_heads(attended_grad, HEAD_DIM), logsum))
        query_part = merge_heads(query_part)
        key_part = merge_heads(key_part)
        value_part = merge_heads(value_part)
        sums_here = partial_sums(attended, stream_grad, normed, clip_mgrad, clip_query, query_scale, query_part, clip_key, key_scale, key_part)
        return (stream_grad.astype(jnp.bfloat16), norm_backward(clip_query, query_scale, norm_gains[0], query_part), norm_backward(clip_key, key_scale, norm_gains[1], key_part), value_part.astype(jnp.bfloat16), sums_here)
    results = lax.map(clip_pass, (clip_major(residual), clip_major(query_raw), clip_major(key_raw), clip_major(values), clip_major(residual_grad), clip_major(modulated_grad), condition))
    return (row_major(results[0]), row_major(results[1]), row_major(results[2]), row_major(results[3]), lax.optimization_barrier(jnp.sum(results[4], axis=0)) * ROWS ** (-0.5))
```

```python
import functools

import jax
import jax.numpy as jnp
from jax import lax
from jax.experimental import pallas as pl
from jax.experimental.pallas import tpu as pltpu
from jax.sharding import PartitionSpec as P

HEAD_DIM = 128
N_SEQ = 4
Z, Y = 8, 4
EPSILON = 1e-06
SCORE_SCALE = HEAD_DIM ** (-0.5)
MESH = pl.DeviceIdType.MESH
VMEM = pltpu.VMEM


def dp_partner(stage, k):
    d = lax.axis_index("dp")
    if stage == "z":
        return (d // Z) * Z + (d % Z + k) % Z
    if stage == "y":
        row = (d // Z) % Y
        return d + ((row + k) % Y - row) * Z
    return (d + Z * Y) % (2 * Z * Y)


STAGES = (("z", Z - 1), ("y", Y - 1), ("x", 1))


def all_partners():
    s = lax.axis_index("seq")
    found = [{"seq": (s + k) % N_SEQ} for k in range(1, N_SEQ)]
    for stage, count in STAGES:
        found += [{"dp": dp_partner(stage, k)} for k in range(1, count + 1)]
    return found


def enter(partners):
    barrier = pltpu.get_barrier_semaphore()
    for partner in partners:
        pl.semaphore_signal(barrier, inc=1, device_id=partner, device_id_type=MESH)
    pl.semaphore_wait(barrier, len(partners))


def dp_sum(stages, start, bufs, sums, send, recv, base):
    current = start
    for index, (stage, count) in enumerate(stages):
        copies = []
        for k in range(1, count + 1):
            copies.append(
                pltpu.make_async_remote_copy(
                    src_ref=current,
                    dst_ref=bufs[stage].at[k - 1],
                    send_sem=send.at[base],
                    recv_sem=recv.at[base],
                    device_id={"dp": dp_partner(stage, k)},
                    device_id_type=MESH,
                )
            )
            base += 1
            copies[-1].start()
        total = current[...]
        for k, copy in enumerate(copies):
            copy.wait_recv()
            total = total + bufs[stage][k]
        sums[index][...] = total
        for copy in copies:
            copy.wait_send()
        current = sums[index]
    return current


def gather_kernel(x_ref, out_ref, zb, yb, xb, s0, s1, s2, full, send, recv):
    s = lax.axis_index("seq")
    enter(all_partners())
    width = x_ref.shape[1]
    mine = dp_sum(STAGES, x_ref, {"z": zb, "y": yb, "x": xb}, (s0, s1, s2), send, recv, 0)
    base = sum(count for _, count in STAGES)
    copies = []
    for k in range(1, N_SEQ):
        copies.append(
            pltpu.make_async_remote_copy(
                src_ref=mine,
                dst_ref=full.at[s],
                send_sem=send.at[base],
                recv_sem=recv.at[base],
                device_id={"seq": (s + k) % N_SEQ},
                device_id_type=MESH,
            )
        )
        base += 1
        copies[-1].start()
    full[s] = mine[...]
    for copy in copies:
        copy.wait()
    for part in range(N_SEQ):
        out_ref[:, part * width : (part + 1) * width] = full[part]


def stage_scratch(width, extra):
    count = sum(c for _, c in STAGES) + N_SEQ - 1
    return [
        VMEM((Z - 1, 8, width), jnp.float32),
        VMEM((Y - 1, 8, width), jnp.float32),
        VMEM((1, 8, width), jnp.float32),
        VMEM((8, width), jnp.float32),
        VMEM((8, width), jnp.float32),
        VMEM((8, width), jnp.float32),
        *extra,
        pltpu.SemaphoreType.DMA((count,)),
        pltpu.SemaphoreType.DMA((count,)),
    ]


def gather_rows(placed):
    width = placed.shape[1]
    return pl.pallas_call(
        gather_kernel,
        out_shape=jax.ShapeDtypeStruct((8, width * N_SEQ), jnp.float32),
        in_specs=[pl.BlockSpec(memory_space=VMEM)],
        out_specs=pl.BlockSpec(memory_space=VMEM),
        scratch_shapes=stage_scratch(width, [VMEM((N_SEQ, 8, width), jnp.float32)]),
        compiler_params=pltpu.CompilerParams(collective_id=0, has_side_effects=True),
    )(placed)


def reduce_kernel(x_ref, out_ref, zb, yb, xb, s0, s1, s2, first, parts, send, recv):
    s = lax.axis_index("seq")
    width = out_ref.shape[1]
    enter(all_partners())
    copies = []
    for k in range(1, N_SEQ):
        p = (s + k) % N_SEQ
        copies.append(
            pltpu.make_async_remote_copy(
                src_ref=x_ref.at[:, pl.ds(pl.multiple_of(p * width, 128), width)],
                dst_ref=parts.at[k - 1],
                send_sem=send.at[k - 1],
                recv_sem=recv.at[k - 1],
                device_id={"seq": p},
                device_id_type=MESH,
            )
        )
        copies[-1].start()
    total = x_ref[:, pl.ds(pl.multiple_of(s * width, 128), width)]
    for k, copy in enumerate(copies):
        copy.wait_recv()
        total = total + parts[k]
    first[...] = total
    for copy in copies:
        copy.wait_send()
    last = dp_sum(
        STAGES[::-1], first, {"z": zb, "y": yb, "x": xb}, (s0, s1, s2), send, recv, N_SEQ - 1
    )
    out_ref[...] = last[...]


def reduce_rows(rows):
    width = rows.shape[1] // N_SEQ
    return pl.pallas_call(
        reduce_kernel,
        out_shape=jax.ShapeDtypeStruct((8, width), jnp.float32),
        in_specs=[pl.BlockSpec(memory_space=VMEM)],
        out_specs=pl.BlockSpec(memory_space=VMEM),
        scratch_shapes=stage_scratch(
            width, [VMEM((8, width), jnp.float32), VMEM((N_SEQ - 1, 8, width), jnp.float32)]
        ),
        compiler_params=pltpu.CompilerParams(collective_id=1, has_side_effects=True),
    )(rows)


def dot_nt(a, b):
    return lax.dot_general(a, b, (((1,), (1,)), ((), ())), preferred_element_type=jnp.float32)


def dot_nn(a, b):
    return lax.dot_general(a, b, (((1,), (0,)), ((), ())), preferred_element_type=jnp.float32)


BLOCK = 256


def forward_kernel(q_ref, k_ref, v_ref, o_ref, stat_ref):
    keys = k_ref[...]
    values_t = v_ref[...].T

    @pl.loop(0, q_ref.shape[0] // BLOCK)
    def _(i):
        rows = pl.ds(pl.multiple_of(i * BLOCK, BLOCK), BLOCK)
        scores = dot_nt(keys, q_ref[rows, :]) * SCORE_SCALE
        top = jnp.max(scores, axis=0, keepdims=True)
        raised = jnp.exp(scores - top)
        total = jnp.sum(raised, axis=0, keepdims=True)
        weights = (raised * (1.0 / total)).astype(jnp.bfloat16)
        attended_t = dot_nn(values_t, weights)
        o_ref[rows, :] = attended_t.T.astype(jnp.bfloat16)
        stat_ref[0, :, rows] = top + jnp.log(total)


def backward_kernel(q_ref, k_ref, v_ref, o_ref, g_ref, stat_ref, dq_ref, dk_ref, dv_ref):
    keys = k_ref[...]
    keys_t = keys.T
    head_values = v_ref[...]
    dk_ref[...] = jnp.zeros_like(dk_ref)
    dv_ref[...] = jnp.zeros_like(dv_ref)

    @pl.loop(0, q_ref.shape[0] // BLOCK)
    def _(i):
        rows = pl.ds(pl.multiple_of(i * BLOCK, BLOCK), BLOCK)
        queries = q_ref[rows, :]
        grads = g_ref[rows, :]
        scores = dot_nt(keys, queries) * SCORE_SCALE
        weights = jnp.exp(scores - stat_ref[0, :, rows])
        product = grads.astype(jnp.float32) * o_ref[rows, :].astype(jnp.float32)
        row_dot = jnp.sum(product.T, axis=0, keepdims=True)
        weight_grad = dot_nt(head_values, grads)
        score_grad = (weights * (weight_grad - row_dot) * SCORE_SCALE).astype(jnp.bfloat16)
        dv_ref[...] += dot_nn(weights.astype(jnp.bfloat16), grads)
        dk_ref[...] += dot_nn(score_grad, queries)
        dq_ref[rows, :] = dot_nn(keys_t, score_grad).T


def head_spec(rows):
    return pl.BlockSpec((rows, HEAD_DIM), lambda h: (0, h))


def head_forward(q, k, v):
    rows, width = q.shape
    heads = width // HEAD_DIM
    return pl.pallas_call(
        forward_kernel,
        grid=(heads,),
        out_shape=(
            jax.ShapeDtypeStruct((rows, width), jnp.bfloat16),
            jax.ShapeDtypeStruct((heads, 1, rows), jnp.float32),
        ),
        in_specs=[head_spec(rows)] * 3,
        out_specs=(head_spec(rows), pl.BlockSpec((1, 1, rows), lambda h: (h, 0, 0))),
        compiler_params=pltpu.CompilerParams(vmem_limit_bytes=40 << 20),
    )(q, k, v)


def head_backward(q, k, v, o, g, stat):
    rows, width = q.shape
    heads = width // HEAD_DIM
    return pl.pallas_call(
        backward_kernel,
        grid=(heads,),
        out_shape=(jax.ShapeDtypeStruct((rows, width), jnp.float32),) * 3,
        in_specs=[head_spec(rows)] * 5 + [pl.BlockSpec((1, 1, rows), lambda h: (h, 0, 0))],
        out_specs=(head_spec(rows),) * 3,
        compiler_params=pltpu.CompilerParams(vmem_limit_bytes=40 << 20),
    )(q, k, v, o, g, stat)


def root_scale(raw_values):
    floats = raw_values.astype(jnp.float32)
    return lax.rsqrt(jnp.mean(floats * floats, axis=1, keepdims=True) + EPSILON)


def stream_pass(residual, attended, modulated, residual_grad, modulated_grad):
    gate_row = modulated[0]
    scale_row = modulated[1]
    summed = residual.astype(jnp.float32) + gate_row * attended.astype(jnp.float32)
    centered = summed - jnp.mean(summed, axis=1, keepdims=True)
    norm_scale = lax.rsqrt(jnp.mean(centered * centered, axis=1, keepdims=True) + EPSILON)
    normed = centered * norm_scale
    scaled_grad = modulated_grad.astype(jnp.float32) * (1.0 + scale_row)
    stream_grad = residual_grad.astype(jnp.float32) + norm_scale * (
        scaled_grad
        - jnp.mean(scaled_grad, axis=1, keepdims=True)
        - normed * jnp.mean(scaled_grad * normed, axis=1, keepdims=True)
    )
    attended_grad = (stream_grad * gate_row).astype(jnp.bfloat16)
    return (stream_grad, normed, attended_grad)


def norm_backward(raw_values, inverse, gain_row, upstream):
    floats = raw_values.astype(jnp.float32)
    weighted = gain_row * upstream
    return (
        inverse * weighted
        - floats * inverse**3 * jnp.mean(floats * weighted, axis=1, keepdims=True)
    ).astype(jnp.bfloat16)


def to_heads(x):
    return lax.all_to_all(x, "seq", split_axis=1, concat_axis=0, tiled=True)


def to_tokens(x):
    return lax.all_to_all(x, "seq", split_axis=0, concat_axis=1, tiled=True)


def per_device(
    residual,
    query_raw,
    key_raw,
    values,
    residual_grad,
    modulated_grad,
    condition,
    modulation,
    norm_gains,
):
    row_count, width = residual.shape
    own = modulation.shape[1]
    d = lax.axis_index("dp")
    placed = lax.dynamic_update_slice(
        jnp.zeros((8, width // N_SEQ), jnp.float32),
        jnp.concatenate([modulation, norm_gains], axis=0),
        (0, d * own),
    )
    params = gather_rows(placed)
    modulated = params[0:2] + condition[0]
    gains = params[2:4]
    query_scale = root_scale(query_raw)
    key_scale = root_scale(key_raw)
    normed_query = (query_raw.astype(jnp.float32) * query_scale * gains[0]).astype(jnp.bfloat16)
    normed_key = (key_raw.astype(jnp.float32) * key_scale * gains[1]).astype(jnp.bfloat16)
    value_heads = to_heads(values)
    query_heads = to_heads(normed_query)
    key_heads = to_heads(normed_key)
    attended_heads, stat = head_forward(query_heads, key_heads, value_heads)
    attended = to_tokens(attended_heads)
    stream_grad, normed, attended_grad = stream_pass(
        residual, attended, modulated, residual_grad, modulated_grad
    )
    query_part, key_part, value_part = head_backward(
        query_heads, key_heads, value_heads, attended_heads, to_heads(attended_grad), stat
    )
    value_grad = to_tokens(value_part.astype(jnp.bfloat16))
    query_grad_n = to_tokens(query_part.astype(jnp.bfloat16)).astype(jnp.float32)
    key_grad_n = to_tokens(key_part.astype(jnp.bfloat16)).astype(jnp.float32)
    grad_floats = modulated_grad.astype(jnp.float32)
    sums_here = jnp.stack(
        [
            jnp.sum(stream_grad * attended.astype(jnp.float32), axis=0),
            jnp.sum(grad_floats, axis=0),
            jnp.sum(grad_floats * normed, axis=0),
            jnp.sum(query_grad_n * query_raw.astype(jnp.float32) * query_scale, axis=0),
            jnp.sum(key_grad_n * key_raw.astype(jnp.float32) * key_scale, axis=0),
        ]
    )
    reduced = reduce_rows(jnp.pad(sums_here, ((0, 3), (0, 0))))
    factor = (row_count * lax.axis_size("seq") * lax.axis_size("dp")) ** (-0.5)
    return (
        stream_grad.astype(jnp.bfloat16),
        norm_backward(query_raw, query_scale, gains[0], query_grad_n),
        norm_backward(key_raw, key_scale, gains[1], key_grad_n),
        value_grad,
        lax.dynamic_slice(reduced, (0, d * own), (5, own)) * factor,
    )


def solution(mesh):
    rows = P(("seq", "dp"), None)
    columns = P(None, ("seq", "dp"))
    return jax.shard_map(
        per_device,
        mesh=mesh,
        in_specs=(rows,) * 6 + (P("dp", None, None), columns, columns),
        out_specs=(rows,) * 4 + (columns,),
        check_vma=False,
    )
```

```python
import functools

import jax
import jax.numpy as jnp
from jax import lax
from jax.experimental import pallas as pl
from jax.experimental.pallas import tpu as pltpu
from jax.sharding import PartitionSpec as P

HEAD_DIM = 128
N_SEQ = 4
EPSILON = 1e-06
SCORE_SCALE = HEAD_DIM ** (-0.5)
MESH = pl.DeviceIdType.MESH
VMEM = pltpu.VMEM
DMA = pltpu.SemaphoreType.DMA
F32 = jnp.float32
BF16 = jnp.bfloat16
BLOCK = 256
CHUNK = 16


def dot_nt(a, b):
    return lax.dot_general(a, b, (((1,), (1,)), ((), ())), preferred_element_type=F32)


def dot_nn(a, b):
    return lax.dot_general(a, b, (((1,), (0,)), ((), ())), preferred_element_type=F32)


def times(start, width):
    return pl.ds(pl.multiple_of(start, width), width)


def kernel(
    layout,
    placed_ref,
    condition_ref,
    residual_hbm,
    query_hbm,
    key_hbm,
    value_hbm,
    residual_grad_hbm,
    modulated_grad_hbm,
    input_grad_hbm,
    query_grad_hbm,
    key_grad_hbm,
    value_grad_hbm,
    sums_ref,
    residual_t,
    query_t,
    key_t,
    residual_grad_t,
    modulated_grad_t,
    attended_t,
    attended_grad_t,
    input_grad_t,
    query_out_t,
    key_out_t,
    scale_t,
    scale_out,
    query_back,
    key_back,
    query_own,
    key_own,
    modulated,
    query_h,
    key_h,
    value_h,
    scale_in,
    scale_h,
    query_n,
    key_n,
    weights_h,
    attended_h,
    grad_h,
    query_grad_h,
    key_grad_h,
    value_grad_h,
    query_total,
    key_total,
    value_total,
    gain_sums,
    zb,
    yb,
    xb,
    gather_sums,
    full,
    zr,
    yr,
    xr,
    reduce_sums,
    columns,
    column_rows,
    seq_parts,
    in_sem,
    own_sem,
    raw_send,
    raw_recv,
    scale_send,
    scale_recv,
    att_send,
    att_recv,
    grad_send,
    grad_recv,
    back_send,
    back_recv,
    gather_send,
    gather_recv,
    reduce_send,
    reduce_recv,
    out_sem,
    value_sem,
):
    n_z, n_y, n_x = layout
    stages = (("z", n_z - 1), ("y", n_y - 1), ("x", n_x - 1))
    dp_count = sum(count for _, count in stages)
    rows, width = residual_t.shape
    heads = query_h.shape[0]
    local = heads * HEAD_DIM
    tokens = query_h.shape[1]
    s = lax.axis_index("seq")
    d = lax.axis_index("dp")
    hops = range(1, N_SEQ)

    def peer(k):
        return (s + k) % N_SEQ

    def sender(k):
        return (s + N_SEQ - k) % N_SEQ

    def dp_partner(stage, k):
        if stage == "z":
            return (d // n_z) * n_z + (d % n_z + k) % n_z
        if stage == "y":
            row = (d // n_z) % n_y
            return d + ((row + k) % n_y - row) * n_z
        return (d + n_z * n_y * k) % (n_z * n_y * n_x)

    def send(src, dst, send_sem, recv_sem, device):
        return pltpu.make_async_remote_copy(
            src_ref=src,
            dst_ref=dst,
            send_sem=send_sem,
            recv_sem=recv_sem,
            device_id=device,
            device_id_type=MESH,
        )

    def head_columns(owner, h):
        return times((owner * heads + h) * HEAD_DIM, HEAD_DIM)

    def token_rows(owner):
        return times(owner * rows, rows)

    raw_hbm = (key_hbm, query_hbm, value_hbm)
    raw_heads = (key_h, query_h, value_h)

    def raw_copy(t, h, k):
        return send(
            raw_hbm[t].at[:, head_columns(peer(k), h)],
            raw_heads[t].at[h, token_rows(s), :],
            raw_send.at[t, h, k - 1],
            raw_recv.at[t, h, k - 1],
            {"seq": peer(k)},
        )

    def own_copy(t, h):
        return pltpu.make_async_copy(
            raw_hbm[t].at[:, head_columns(s, h)],
            raw_heads[t].at[h, token_rows(s), :],
            own_sem.at[t, h],
        )

    def scale_copy(k):
        return send(
            scale_out,
            scale_in.at[s],
            scale_send.at[k - 1],
            scale_recv.at[k - 1],
            {"seq": peer(k)},
        )

    def att_copy(h, k):
        return send(
            attended_h.at[h, token_rows(peer(k)), :],
            attended_t.at[:, head_columns(s, h)],
            att_send.at[h, k - 1],
            att_recv.at[h, k - 1],
            {"seq": peer(k)},
        )

    def grad_copy(h, k):
        return send(
            attended_grad_t.at[:, head_columns(peer(k), h)],
            grad_h.at[h, token_rows(s), :],
            grad_send.at[h, k - 1],
            grad_recv.at[h, k - 1],
            {"seq": peer(k)},
        )

    def back_copy(t, h, k):
        if t == 2:
            src, dst = value_grad_h, value_grad_hbm.at[:, head_columns(s, h)]
        else:
            src = (query_grad_h, key_grad_h)[t]
            dst = (query_back, key_back)[t].at[k - 1, :, times(h * HEAD_DIM, HEAD_DIM)]
        return send(
            src.at[h, token_rows(peer(k)), :],
            dst,
            back_send.at[t, h, k - 1],
            back_recv.at[t, h, k - 1],
            {"seq": peer(k)},
        )

    def value_copy(h):
        return pltpu.make_async_copy(
            value_grad_h.at[h, token_rows(s), :],
            value_grad_hbm.at[:, head_columns(s, h)],
            value_sem.at[h],
        )

    def start_raw(h):
        for t in range(3):
            for k in hops:
                raw_copy(t, h, k).start()

    def dp_sum(order, start, bufs, totals, send_sem, recv_sem, base, beside):
        current = start
        sent = []
        for index, (stage, count) in enumerate(order):
            copies = [
                send(
                    current,
                    bufs[stage].at[k - 1],
                    send_sem.at[base + k - 1],
                    recv_sem.at[base + k - 1],
                    {"dp": dp_partner(stage, k)},
                )
                for k in range(1, count + 1)
            ]
            base += count
            for copy in copies:
                copy.start()
            beside(index)
            total = current[...]
            for k, copy in enumerate(copies):
                copy.wait_recv()
                total = total + bufs[stage][k]
            totals[index] = total
            sent += copies
            current = totals.at[index]
        return current, sent

    inputs = (
        (key_hbm, key_t),
        (query_hbm, query_t),
        (residual_hbm, residual_t),
        (residual_grad_hbm, residual_grad_t),
        (modulated_grad_hbm, modulated_grad_t),
    )
    loads = [
        pltpu.make_async_copy(src, dst, in_sem.at[i]) for i, (src, dst) in enumerate(inputs)
    ]
    for load in loads:
        load.start()
    for t in range(3):
        for h in range(heads):
            own_copy(t, h).start()

    partners = [{"seq": peer(k)} for k in hops]
    for stage, count in stages:
        partners += [{"dp": dp_partner(stage, k)} for k in range(1, count + 1)]
    barrier = pltpu.get_barrier_semaphore()
    for partner in partners:
        pl.semaphore_signal(barrier, inc=1, device_id=partner, device_id_type=MESH)
    pl.semaphore_wait(barrier, len(partners))

    def scales():
        scale_t[:, rows:, :] = jnp.zeros((2, BLOCK - rows, HEAD_DIM), F32)
        for t, source in ((0, key_t), (1, query_t)):
            loads[t].wait()

            @pl.loop(0, rows // CHUNK)
            def _(i):
                at = times(i * CHUNK, CHUNK)
                floats = source[at, :].astype(F32)
                mean = jnp.sum(floats * floats, axis=1, keepdims=True) * (1.0 / width)
                scale_t[t, at, :] = jnp.broadcast_to(
                    lax.rsqrt(mean + EPSILON), (CHUNK, HEAD_DIM)
                )

            scale_out[t] = scale_t[t].T[0:8, :]
        for k in hops:
            scale_copy(k).start()
        scale_in[s] = scale_out[...]

    def beside_gather(index):
        start_raw(index)
        if index == 0:
            scales()

    mine, gather_copies = dp_sum(
        stages,
        placed_ref,
        {"z": zb, "y": yb, "x": xb},
        gather_sums,
        gather_send,
        gather_recv,
        0,
        beside_gather,
    )
    full[s] = mine[...]
    full_copies = [
        send(
            mine,
            full.at[s],
            gather_send.at[dp_count + k - 1],
            gather_recv.at[dp_count + k - 1],
            {"seq": peer(k)},
        )
        for k in hops
    ]
    for copy in full_copies:
        copy.start()
    for h in range(len(stages), heads):
        start_raw(h)

    for k in hops:
        scale_copy(k).wait_recv()
    for owner in range(N_SEQ):
        for t in range(2):
            spread = jnp.broadcast_to(scale_in[owner, t, 0:1, :], (HEAD_DIM, BLOCK)).T
            scale_h[t, owner * rows : (owner + 1) * rows, :] = spread[0:rows, :]

    @pl.loop(0, heads)
    def _(h):
        gain_at = times(h * HEAD_DIM, HEAD_DIM)
        for t in range(3):
            own_copy(t, h).wait()
            for k in hops:
                raw_copy(t, h, k).wait_recv()
        query_n[h] = (query_h[h].astype(F32) * scale_h[1] * mine[2:3, gain_at]).astype(BF16)
        key_n[h] = (key_h[h].astype(F32) * scale_h[0] * mine[3:4, gain_at]).astype(BF16)
        values_t = value_h[h].T

        @pl.loop(0, tokens // BLOCK)
        def _(i):
            at = times(i * BLOCK, BLOCK)
            scores = dot_nt(key_n[h], query_n[h, at, :]) * SCORE_SCALE
            top = jnp.max(scores, axis=0, keepdims=True)
            raised = jnp.exp(scores - top)
            total = jnp.sum(raised, axis=0, keepdims=True)
            weights = raised * (1.0 / total)
            weights_h[h, :, at] = weights
            attended_h[h, at, :] = dot_nn(values_t, weights.astype(BF16)).T.astype(BF16)

        for k in hops:
            att_copy(h, k).start()
        attended_t[:, head_columns(s, h)] = attended_h[h, token_rows(s), :]

    for copy in full_copies:
        copy.wait_recv()
    for part in range(N_SEQ):
        at = slice(part * local, (part + 1) * local)
        modulated[:, at] = full[part, 0:2, :] + condition_ref[:, at]
    for load in loads[2:]:
        load.wait()
    columns[...] = jnp.zeros_like(columns)

    @pl.loop(0, heads)
    def _(h):
        for k in hops:
            att_copy(h, k).wait_recv()

    @pl.loop(0, rows // CHUNK)
    def _(i):
        at = times(i * CHUNK, CHUNK)
        gate_row = modulated[0:1, :]
        attended = attended_t[at, :].astype(F32)
        summed = residual_t[at, :].astype(F32) + gate_row * attended
        centered = summed - jnp.sum(summed, axis=1, keepdims=True) * (1.0 / width)
        norm_scale = lax.rsqrt(
            jnp.sum(centered * centered, axis=1, keepdims=True) * (1.0 / width) + EPSILON
        )
        normed = centered * norm_scale
        upstream = modulated_grad_t[at, :].astype(F32)
        scaled = upstream * (1.0 + modulated[1:2, :])
        stream_grad = residual_grad_t[at, :].astype(F32) + norm_scale * (
            scaled
            - jnp.sum(scaled, axis=1, keepdims=True) * (1.0 / width)
            - normed * (jnp.sum(scaled * normed, axis=1, keepdims=True) * (1.0 / width))
        )
        input_grad_t[at, :] = stream_grad.astype(BF16)
        attended_grad_t[at, :] = (stream_grad * gate_row).astype(BF16)
        for row, term in enumerate((stream_grad * attended, upstream, upstream * normed)):
            columns[row] += term[0:8, :] + term[8:16, :]

    @pl.loop(0, heads)
    def _(h):
        for k in hops:
            grad_copy(h, k).start()
        grad_h[h, token_rows(s), :] = attended_grad_t[:, head_columns(s, h)]

    input_grad_out = pltpu.make_async_copy(input_grad_t, input_grad_hbm, out_sem.at[0])
    input_grad_out.start()
    column_rows[3:8, :] = jnp.zeros((5, width), F32)
    for row in range(3):
        column_rows[row : row + 1, :] = jnp.sum(columns[row], axis=0, keepdims=True)
    seq_copies = [
        send(
            column_rows.at[:, times(peer(k) * local, HEAD_DIM * heads)],
            seq_parts.at[k - 1],
            reduce_send.at[dp_count + k - 1],
            reduce_recv.at[dp_count + k - 1],
            {"seq": peer(k)},
        )
        for k in hops
    ]
    for copy in seq_copies:
        copy.start()
    gain_sums[0:3, :] = column_rows[0:3, times(s * local, HEAD_DIM * heads)]
    gain_sums[5:8, :] = jnp.zeros((3, local), F32)

    @pl.loop(0, heads)
    def _(h):
        for k in hops:
            grad_copy(h, k).wait_recv()
        at_head = times(h * HEAD_DIM, HEAD_DIM)
        keys_t = key_n[h].T
        key_total[...] = jnp.zeros_like(key_total)
        value_total[...] = jnp.zeros_like(value_total)
        gain_sums[3:4, at_head] = jnp.zeros((1, HEAD_DIM), F32)

        @pl.loop(0, tokens // BLOCK)
        def _(i):
            at = times(i * BLOCK, BLOCK)
            queries = query_n[h, at, :]
            grads = grad_h[h, at, :]
            weights = weights_h[h, :, at]
            product = grads.astype(F32) * attended_h[h, at, :].astype(F32)
            row_dot = jnp.sum(product.T, axis=0, keepdims=True)
            weight_grad = dot_nt(value_h[h], grads)
            score_grad = (weights * (weight_grad - row_dot) * SCORE_SCALE).astype(BF16)
            value_total[...] += dot_nn(weights.astype(BF16), grads)
            key_total[...] += dot_nn(score_grad, queries)
            query_grad = dot_nn(keys_t, score_grad).T
            query_total[at, :] = query_grad
            query_grad_h[h, at, :] = query_grad.astype(BF16)
            gain_sums[3:4, at_head] += jnp.sum(
                query_grad * (query_h[h, at, :].astype(F32) * scale_h[1, at, :]),
                axis=0,
                keepdims=True,
            )

        key_grad_h[h] = key_total[...].astype(BF16)
        value_grad_h[h] = value_total[...].astype(BF16)
        gain_sums[4:5, at_head] = jnp.sum(
            key_total[...] * (key_h[h].astype(F32) * scale_h[0]), axis=0, keepdims=True
        )
        for t in range(3):
            for k in hops:
                back_copy(t, h, k).start()
        value_copy(h).start()
        query_own[:, at_head] = query_total[token_rows(s), :]
        key_own[:, at_head] = key_total[token_rows(s), :]

    for k, copy in enumerate(seq_copies):
        copy.wait_recv()
        gain_sums[0:3, :] += seq_parts[k, 0:3, :]
    reduced, reduce_copies = dp_sum(
        stages[::-1],
        gain_sums,
        {"z": zr, "y": yr, "x": xr},
        reduce_sums,
        reduce_send,
        reduce_recv,
        0,
        lambda index: None,
    )
    sums_ref[...] = reduced[...]

    outs = []
    for t, (raw, back, own, out, out_hbm, scale_row, gain_row) in enumerate(
        (
            (query_t, query_back, query_own, query_out_t, query_grad_hbm, 1, 2),
            (key_t, key_back, key_own, key_out_t, key_grad_hbm, 0, 3),
        )
    ):

        @pl.loop(0, heads)
        def _(h):
            for k in hops:
                back_copy(t, h, k).wait_recv()

        @pl.loop(0, rows // CHUNK)
        def _(i):
            at = times(i * CHUNK, CHUNK)
            inverse = scale_t[scale_row, at, 0:1]
            parts = []
            mean = jnp.zeros((CHUNK, 1), F32)
            for k in range(N_SEQ):
                block = sender(k)
                where = times(block * local, HEAD_DIM * heads)
                upstream = own[at, :] if k == 0 else back[k - 1, at, :].astype(F32)
                weighted = full[block, gain_row : gain_row + 1, :] * upstream
                floats = raw[at, where].astype(F32)
                mean = mean + jnp.sum(floats * weighted, axis=1, keepdims=True)
                parts.append((where, weighted, floats))
            factor = inverse * inverse * inverse * (mean * (1.0 / width))
            for where, weighted, floats in parts:
                out[at, where] = (inverse * weighted - floats * factor).astype(BF16)

        outs.append(pltpu.make_async_copy(out, out_hbm, out_sem.at[1 + t]))
        outs[-1].start()

    @pl.loop(0, heads)
    def _(h):
        for t in range(3):
            for k in hops:
                raw_copy(t, h, k).wait_send()
                back_copy(t, h, k).wait_send()
        for k in hops:
            back_copy(2, h, k).wait_recv()
            att_copy(h, k).wait_send()
            grad_copy(h, k).wait_send()
        value_copy(h).wait()

    for k in hops:
        scale_copy(k).wait_send()
    for copy in gather_copies + full_copies + seq_copies + reduce_copies:
        copy.wait_send()
    input_grad_out.wait()
    for out in outs:
        out.wait()


def whole_block(layout, placed, condition, residual, query, key, value, residual_grad, mod_grad):
    rows, width = residual.shape
    local = width // N_SEQ
    heads = local // HEAD_DIM
    tokens = rows * N_SEQ
    n_z, n_y, n_x = layout
    dp_count = n_z + n_y + n_x - 3
    token = VMEM((rows, width), BF16)
    by_head = VMEM((heads, tokens, HEAD_DIM), BF16)

    def stage_bufs():
        return [VMEM((max(n - 1, 1), 8, local), F32) for n in layout]

    hbm = pl.BlockSpec(memory_space=pl.ANY)
    vmem = pl.BlockSpec(memory_space=VMEM)
    big = jax.ShapeDtypeStruct((rows, width), BF16)
    hops = N_SEQ - 1
    return pl.pallas_call(
        functools.partial(kernel, layout),
        out_shape=(big, big, big, big, jax.ShapeDtypeStruct((8, local), F32)),
        in_specs=[vmem, vmem] + [hbm] * 6,
        out_specs=(hbm, hbm, hbm, hbm, vmem),
        scratch_shapes=[
            token,
            token,
            token,
            token,
            token,
            token,
            token,
            token,
            token,
            token,
            VMEM((2, BLOCK, HEAD_DIM), F32),
            VMEM((2, 8, BLOCK), F32),
            VMEM((hops, rows, local), BF16),
            VMEM((hops, rows, local), BF16),
            VMEM((rows, local), F32),
            VMEM((rows, local), F32),
            VMEM((2, width), F32),
            by_head,
            by_head,
            by_head,
            VMEM((N_SEQ, 2, 8, BLOCK), F32),
            VMEM((2, tokens, HEAD_DIM), F32),
            by_head,
            by_head,
            VMEM((heads, tokens, tokens), F32),
            by_head,
            by_head,
            by_head,
            by_head,
            by_head,
            VMEM((tokens, HEAD_DIM), F32),
            VMEM((tokens, HEAD_DIM), F32),
            VMEM((tokens, HEAD_DIM), F32),
            VMEM((8, local), F32),
            *stage_bufs(),
            VMEM((3, 8, local), F32),
            VMEM((N_SEQ, 8, local), F32),
            *stage_bufs(),
            VMEM((3, 8, local), F32),
            VMEM((3, 8, width), F32),
            VMEM((8, width), F32),
            VMEM((hops, 8, local), F32),
            DMA((5,)),
            DMA((3, heads)),
            DMA((3, heads, hops)),
            DMA((3, heads, hops)),
            DMA((hops,)),
            DMA((hops,)),
            DMA((heads, hops)),
            DMA((heads, hops)),
            DMA((heads, hops)),
            DMA((heads, hops)),
            DMA((3, heads, hops)),
            DMA((3, heads, hops)),
            DMA((dp_count + hops,)),
            DMA((dp_count + hops,)),
            DMA((dp_count + hops,)),
            DMA((dp_count + hops,)),
            DMA((3,)),
            DMA((heads,)),
        ],
        compiler_params=pltpu.CompilerParams(
            collective_id=0, has_side_effects=True, vmem_limit_bytes=58 << 20
        ),
    )(placed, condition, residual, query, key, value, residual_grad, mod_grad)


def per_device(
    layout,
    residual,
    query_raw,
    key_raw,
    values,
    residual_grad,
    modulated_grad,
    condition,
    modulation,
    norm_gains,
):
    row_count, width = residual.shape
    own = modulation.shape[1]
    d = lax.axis_index("dp")
    placed = lax.dynamic_update_slice(
        jnp.zeros((8, width // N_SEQ), F32),
        jnp.concatenate([modulation, norm_gains], axis=0),
        (0, d * own),
    )
    input_grad, query_grad, key_grad, value_grad, reduced = whole_block(
        layout,
        placed,
        condition[0],
        residual,
        query_raw,
        key_raw,
        values,
        residual_grad,
        modulated_grad,
    )
    factor = (row_count * lax.axis_size("seq") * lax.axis_size("dp")) ** (-0.5)
    return (
        input_grad,
        query_grad,
        key_grad,
        value_grad,
        lax.dynamic_slice(reduced, (0, d * own), (5, own)) * factor,
    )


def solution(mesh):
    layout = (8, 4, mesh.shape["dp"] // 32) if mesh.shape["dp"] >= 32 else (mesh.shape["dp"], 1, 1)
    rows = P(("seq", "dp"), None)
    columns = P(None, ("seq", "dp"))
    return jax.shard_map(
        functools.partial(per_device, layout),
        mesh=mesh,
        in_specs=(rows,) * 6 + (P("dp", None, None), columns, columns),
        out_specs=(rows,) * 4 + (columns,),
        check_vma=False,
    )
```

```python
import functools

import jax
import jax.numpy as jnp
from jax import lax
from jax.experimental import pallas as pl
from jax.experimental.pallas import tpu as pltpu
from jax.sharding import PartitionSpec as P

HEAD_DIM = 128
N_SEQ = 4
EPSILON = 1e-06
SCORE_SCALE = HEAD_DIM ** (-0.5)
MESH = pl.DeviceIdType.MESH
VMEM = pltpu.VMEM
DMA = pltpu.SemaphoreType.DMA
F32 = jnp.float32
BF16 = jnp.bfloat16
BLOCK = 256
CHUNK = 16
PARTS = ((0, 48), (48, 48), (96, 96))
EARLY = 2
SPLIT = 2


def dot_nt(a, b):
    return lax.dot_general(a, b, (((1,), (1,)), ((), ())), preferred_element_type=F32)


def dot_nn(a, b):
    return lax.dot_general(a, b, (((1,), (0,)), ((), ())), preferred_element_type=F32)


def times(start, width):
    return pl.ds(pl.multiple_of(start, width), width)


def kernel(
    layout,
    modulation_ref,
    gains_ref,
    condition_ref,
    residual_hbm,
    query_hbm,
    key_hbm,
    value_hbm,
    residual_grad_hbm,
    modulated_grad_hbm,
    input_grad_hbm,
    query_grad_hbm,
    key_grad_hbm,
    value_grad_hbm,
    sums_ref,
    residual_t,
    query_t,
    key_t,
    residual_grad_t,
    modulated_grad_t,
    attended_t,
    attended_grad_t,
    input_grad_t,
    query_out_t,
    key_out_t,
    scale_t,
    scale_out,
    query_back,
    key_back,
    query_own,
    key_own,
    modulated,
    query_h,
    key_h,
    value_h,
    scale_in,
    scale_h,
    query_n,
    key_n,
    weights_h,
    attended_h,
    grad_h,
    query_grad_h,
    key_grad_h,
    value_grad_h,
    query_total,
    key_total,
    value_total,
    gain_sums,
    placed,
    zb,
    yb,
    xb,
    gather_sums,
    full,
    zr,
    yr,
    xr,
    reduce_sums,
    columns,
    column_rows,
    seq_parts,
    in_sem,
    own_sem,
    raw_send,
    raw_recv,
    scale_send,
    scale_recv,
    att_send,
    att_recv,
    grad_send,
    grad_recv,
    back_send,
    back_recv,
    gather_send,
    gather_recv,
    reduce_send,
    reduce_recv,
    out_sem,
    value_sem,
):
    n_z, n_y, n_x = layout
    stages = (("z", n_z - 1), ("y", n_y - 1), ("x", n_x - 1))
    dp_count = sum(count for _, count in stages)
    rows, width = residual_t.shape
    heads = query_h.shape[0]
    local = heads * HEAD_DIM
    tokens = query_h.shape[1]
    s = lax.axis_index("seq")
    d = lax.axis_index("dp")
    hops = range(1, N_SEQ)

    def peer(k):
        return (s + k) % N_SEQ

    def sender(k):
        return (s + N_SEQ - k) % N_SEQ

    def dp_partner(stage, k):
        if stage == "z":
            return (d // n_z) * n_z + (d % n_z + k) % n_z
        if stage == "y":
            row = (d // n_z) % n_y
            return d + ((row + k) % n_y - row) * n_z
        return (d + n_z * n_y * k) % (n_z * n_y * n_x)

    def send(src, dst, send_sem, recv_sem, device):
        return pltpu.make_async_remote_copy(
            src_ref=src,
            dst_ref=dst,
            send_sem=send_sem,
            recv_sem=recv_sem,
            device_id=device,
            device_id_type=MESH,
        )

    def head_columns(owner, h):
        return times((owner * heads + h) * HEAD_DIM, HEAD_DIM)

    def token_rows(owner):
        return times(owner * rows, rows)

    raw_hbm = (key_hbm, query_hbm, value_hbm)
    raw_heads = (key_h, query_h, value_h)

    def raw_copy(t, h, k):
        return send(
            raw_hbm[t].at[:, head_columns(peer(k), h)],
            raw_heads[t].at[h, token_rows(s), :],
            raw_send.at[t, h, k - 1],
            raw_recv.at[t, h, k - 1],
            {"seq": peer(k)},
        )

    def own_copy(t, h):
        return pltpu.make_async_copy(
            raw_hbm[t].at[:, head_columns(s, h)],
            raw_heads[t].at[h, token_rows(s), :],
            own_sem.at[t, h],
        )

    def scale_copy(k):
        return send(
            scale_out,
            scale_in.at[s],
            scale_send.at[k - 1],
            scale_recv.at[k - 1],
            {"seq": peer(k)},
        )

    def att_copy(h, k):
        return send(
            attended_h.at[h, token_rows(peer(k)), :],
            attended_t.at[:, head_columns(s, h)],
            att_send.at[h, k - 1],
            att_recv.at[h, k - 1],
            {"seq": peer(k)},
        )

    def part_rows(part):
        first, count = PARTS[part]
        return pl.ds(pl.multiple_of(s * rows + first, CHUNK), count)

    def grad_copy(part, h, k):
        first, count = PARTS[part]
        return send(
            attended_grad_t.at[pl.ds(first, count), head_columns(peer(k), h)],
            grad_h.at[h, part_rows(part), :],
            grad_send.at[part, h, k - 1],
            grad_recv.at[part, h, k - 1],
            {"seq": peer(k)},
        )

    def back_copy(t, h, k):
        if t == 2:
            src, dst = value_grad_h, value_grad_hbm.at[:, head_columns(s, h)]
        else:
            src = (query_grad_h, key_grad_h)[t]
            dst = (query_back, key_back)[t].at[k - 1, :, times(h * HEAD_DIM, HEAD_DIM)]
        return send(
            src.at[h, token_rows(peer(k)), :],
            dst,
            back_send.at[t, h, k - 1],
            back_recv.at[t, h, k - 1],
            {"seq": peer(k)},
        )

    def value_copy(h):
        return pltpu.make_async_copy(
            value_grad_h.at[h, token_rows(s), :],
            value_grad_hbm.at[:, head_columns(s, h)],
            value_sem.at[h],
        )

    def start_raw(h):
        for t in range(3):
            for k in hops:
                raw_copy(t, h, k).start()

    def dp_sum(order, start, bufs, totals, send_sem, recv_sem, base, beside):
        current = start
        sent = []
        for index, (stage, count) in enumerate(order):
            copies = [
                send(
                    current,
                    bufs[stage].at[k - 1],
                    send_sem.at[base + k - 1],
                    recv_sem.at[base + k - 1],
                    {"dp": dp_partner(stage, k)},
                )
                for k in range(1, count + 1)
            ]
            base += count
            for copy in copies:
                copy.start()
            beside(index)
            total = current[...]
            for k, copy in enumerate(copies):
                copy.wait_recv()
                total = total + bufs[stage][k]
            totals[index] = total
            sent += copies
            current = totals.at[index]
        return current, sent

    def start_back(t, h):
        for k in hops:
            back_copy(t, h, k).start()

    inputs = (
        (key_hbm, key_t),
        (query_hbm, query_t),
        (residual_hbm, residual_t),
        (residual_grad_hbm, residual_grad_t),
        (modulated_grad_hbm, modulated_grad_t),
    )
    loads = [
        pltpu.make_async_copy(src, dst, in_sem.at[i]) for i, (src, dst) in enumerate(inputs)
    ]
    for load in loads:
        load.start()
    for t in range(3):
        for h in range(heads):
            own_copy(t, h).start()

    own = modulation_ref.shape[1]
    placed[...] = jnp.zeros_like(placed)
    placed[0:2, 0:own] = modulation_ref[...]
    placed[2:4, 0:own] = gains_ref[...]
    placed[...] = pltpu.roll(placed[...], d * own, 1)

    partners = [{"seq": peer(k)} for k in hops]
    for stage, count in stages:
        partners += [{"dp": dp_partner(stage, k)} for k in range(1, count + 1)]
    barrier = pltpu.get_barrier_semaphore()
    for partner in partners:
        pl.semaphore_signal(barrier, inc=1, device_id=partner, device_id_type=MESH)
    pl.semaphore_wait(barrier, len(partners))

    def scales():
        scale_t[:, rows:, :] = jnp.zeros((2, BLOCK - rows, HEAD_DIM), F32)
        for t, source in ((0, key_t), (1, query_t)):
            loads[t].wait()

            @pl.loop(0, rows // CHUNK)
            def _(i):
                at = times(i * CHUNK, CHUNK)
                floats = source[at, :].astype(F32)
                mean = jnp.sum(floats * floats, axis=1, keepdims=True) * (1.0 / width)
                scale_t[t, at, :] = jnp.broadcast_to(
                    lax.rsqrt(mean + EPSILON), (CHUNK, HEAD_DIM)
                )

            scale_out[t] = scale_t[t].T[0:8, :]
        for k in hops:
            scale_copy(k).start()
        scale_in[s] = scale_out[...]

    def beside_gather(index):
        start_raw(index)
        if index == 0:
            scales()

    mine, gather_copies = dp_sum(
        stages,
        placed,
        {"z": zb, "y": yb, "x": xb},
        gather_sums,
        gather_send,
        gather_recv,
        0,
        beside_gather,
    )
    full[s] = mine[...]
    full_copies = [
        send(
            mine,
            full.at[s],
            gather_send.at[dp_count + k - 1],
            gather_recv.at[dp_count + k - 1],
            {"seq": peer(k)},
        )
        for k in hops
    ]
    for copy in full_copies:
        copy.start()
    for h in range(len(stages), heads):
        start_raw(h)

    for k in hops:
        scale_copy(k).wait_recv()
    for owner in range(N_SEQ):
        for t in range(2):
            spread = jnp.broadcast_to(scale_in[owner, t, 0:1, :], (HEAD_DIM, BLOCK)).T
            scale_h[t, owner * rows : (owner + 1) * rows, :] = spread[0:rows, :]

    @pl.loop(0, heads)
    def _(h):
        gain_at = times(h * HEAD_DIM, HEAD_DIM)
        for t in range(3):
            own_copy(t, h).wait()
            for k in hops:
                raw_copy(t, h, k).wait_recv()
        query_n[h] = (query_h[h].astype(F32) * scale_h[1] * mine[2:3, gain_at]).astype(BF16)
        key_n[h] = (key_h[h].astype(F32) * scale_h[0] * mine[3:4, gain_at]).astype(BF16)
        values_t = value_h[h].T

        @pl.loop(0, tokens // BLOCK)
        def _(i):
            at = times(i * BLOCK, BLOCK)
            scores = dot_nt(key_n[h], query_n[h, at, :]) * SCORE_SCALE
            top = jnp.max(scores, axis=0, keepdims=True)
            raised = jnp.exp(scores - top)
            total = jnp.sum(raised, axis=0, keepdims=True)
            weights = raised * (1.0 / total)
            weights_h[h, :, at] = weights
            attended_h[h, at, :] = dot_nn(values_t, weights.astype(BF16)).T.astype(BF16)

        for k in hops:
            att_copy(h, k).start()
        attended_t[:, head_columns(s, h)] = attended_h[h, token_rows(s), :]

    for copy in full_copies:
        copy.wait_recv()
    for part in range(N_SEQ):
        at = slice(part * local, (part + 1) * local)
        modulated[:, at] = full[part, 0:2, :] + condition_ref[:, at]
    for load in loads[2:]:
        load.wait()
    columns[...] = jnp.zeros_like(columns)

    @pl.loop(0, heads)
    def _(h):
        for k in hops:
            att_copy(h, k).wait_recv()

    for part, (first, count) in enumerate(PARTS):

        @pl.loop(first // CHUNK, (first + count) // CHUNK)
        def _(i):
            at = times(i * CHUNK, CHUNK)
            gate_row = modulated[0:1, :]
            attended = attended_t[at, :].astype(F32)
            summed = residual_t[at, :].astype(F32) + gate_row * attended
            centered = summed - jnp.sum(summed, axis=1, keepdims=True) * (1.0 / width)
            norm_scale = lax.rsqrt(
                jnp.sum(centered * centered, axis=1, keepdims=True) * (1.0 / width) + EPSILON
            )
            normed = centered * norm_scale
            upstream = modulated_grad_t[at, :].astype(F32)
            scaled = upstream * (1.0 + modulated[1:2, :])
            stream_grad = residual_grad_t[at, :].astype(F32) + norm_scale * (
                scaled
                - jnp.sum(scaled, axis=1, keepdims=True) * (1.0 / width)
                - normed * (jnp.sum(scaled * normed, axis=1, keepdims=True) * (1.0 / width))
            )
            input_grad_t[at, :] = stream_grad.astype(BF16)
            attended_grad_t[at, :] = (stream_grad * gate_row).astype(BF16)
            for row, term in enumerate((stream_grad * attended, upstream, upstream * normed)):
                columns[row] += term[0:8, :] + term[8:16, :]

        @pl.loop(0, heads)
        def _(h):
            for k in hops:
                grad_copy(part, h, k).start()
            grad_h[h, part_rows(part), :] = attended_grad_t[
                first : first + count, head_columns(s, h)
            ]

    input_grad_out = pltpu.make_async_copy(input_grad_t, input_grad_hbm, out_sem.at[0])
    input_grad_out.start()
    column_rows[3:8, :] = jnp.zeros((5, width), F32)
    for row in range(3):
        column_rows[row : row + 1, :] = jnp.sum(columns[row], axis=0, keepdims=True)
    seq_copies = [
        send(
            column_rows.at[:, times(peer(k) * local, HEAD_DIM * heads)],
            seq_parts.at[k - 1],
            reduce_send.at[dp_count + k - 1],
            reduce_recv.at[dp_count + k - 1],
            {"seq": peer(k)},
        )
        for k in hops
    ]
    for copy in seq_copies:
        copy.start()
    gain_sums[0:3, :] = column_rows[0:3, times(s * local, HEAD_DIM * heads)]
    gain_sums[5:8, :] = jnp.zeros((3, local), F32)

    @pl.loop(0, heads)
    def _(h):
        for part in range(len(PARTS)):
            for k in hops:
                grad_copy(part, h, k).wait_recv()
        at_head = times(h * HEAD_DIM, HEAD_DIM)
        keys_t = key_n[h].T
        key_total[...] = jnp.zeros_like(key_total)
        value_total[...] = jnp.zeros_like(value_total)
        gain_sums[3:4, at_head] = jnp.zeros((1, HEAD_DIM), F32)

        @pl.loop(0, tokens // BLOCK)
        def _(i):
            at = times(i * BLOCK, BLOCK)
            queries = query_n[h, at, :]
            grads = grad_h[h, at, :]
            weights = weights_h[h, :, at]
            product = grads.astype(F32) * attended_h[h, at, :].astype(F32)
            row_dot = jnp.sum(product.T, axis=0, keepdims=True)
            weight_grad = dot_nt(value_h[h], grads)
            score_grad = (weights * (weight_grad - row_dot) * SCORE_SCALE).astype(BF16)
            value_total[...] += dot_nn(weights.astype(BF16), grads)
            key_total[...] += dot_nn(score_grad, queries)
            query_grad = dot_nn(keys_t, score_grad).T
            query_total[at, :] = query_grad
            query_grad_h[h, at, :] = query_grad.astype(BF16)
            gain_sums[3:4, at_head] += jnp.sum(
                query_grad * (query_h[h, at, :].astype(F32) * scale_h[1, at, :]),
                axis=0,
                keepdims=True,
            )

        key_grad_h[h] = key_total[...].astype(BF16)
        value_grad_h[h] = value_total[...].astype(BF16)
        gain_sums[4:5, at_head] = jnp.sum(
            key_total[...] * (key_h[h].astype(F32) * scale_h[0]), axis=0, keepdims=True
        )

        @pl.when(h < EARLY)
        def _():
            for t in range(3):
                start_back(t, h)

        value_copy(h).start()
        query_own[:, at_head] = query_total[token_rows(s), :]
        key_own[:, at_head] = key_total[token_rows(s), :]

    late = [(t, h) for h in range(EARLY, heads) for t in range(2)]
    late += [(2, h) for h in range(EARLY, heads)]

    def beside_reduce(index):
        per_stage = len(late) // len(stages)
        for t, h in late[index * per_stage : (index + 1) * per_stage]:
            start_back(t, h)

    for k, copy in enumerate(seq_copies):
        copy.wait_recv()
        gain_sums[0:3, :] += seq_parts[k, 0:3, :]
    reduced, reduce_copies = dp_sum(
        stages[::-1],
        gain_sums,
        {"z": zr, "y": yr, "x": xr},
        reduce_sums,
        reduce_send,
        reduce_recv,
        0,
        beside_reduce,
    )
    sums_ref[...] = pltpu.roll(reduced[...], local - d * own, 1)

    outs = []
    for t, (raw, back, own, out, out_hbm, scale_row, gain_row) in enumerate(
        (
            (query_t, query_back, query_own, query_out_t, query_grad_hbm, 1, 2),
            (key_t, key_back, key_own, key_out_t, key_grad_hbm, 0, 3),
        )
    ):

        @pl.loop(0, heads)
        def _(h):
            for k in hops:
                back_copy(t, h, k).wait_recv()

        @pl.loop(0, rows // CHUNK)
        def _(i):
            at = times(i * CHUNK, CHUNK)
            inverse = scale_t[scale_row, at, 0:1]
            parts = []
            mean = jnp.zeros((CHUNK, 1), F32)
            for k in range(N_SEQ):
                block = sender(k)
                where = times(block * local, HEAD_DIM * heads)
                upstream = own[at, :] if k == 0 else back[k - 1, at, :].astype(F32)
                weighted = full[block, gain_row : gain_row + 1, :] * upstream
                floats = raw[at, where].astype(F32)
                mean = mean + jnp.sum(floats * weighted, axis=1, keepdims=True)
                parts.append((where, weighted, floats))
            factor = inverse * inverse * inverse * (mean * (1.0 / width))
            for where, weighted, floats in parts:
                out[at, where] = (inverse * weighted - floats * factor).astype(BF16)

        outs.append(pltpu.make_async_copy(out, out_hbm, out_sem.at[1 + t]))
        outs[-1].start()

    @pl.loop(0, heads)
    def _(h):
        for t in range(3):
            for k in hops:
                raw_copy(t, h, k).wait_send()
                back_copy(t, h, k).wait_send()
        for k in hops:
            back_copy(2, h, k).wait_recv()
            att_copy(h, k).wait_send()
            for part in range(len(PARTS)):
                grad_copy(part, h, k).wait_send()
        value_copy(h).wait()

    for k in hops:
        scale_copy(k).wait_send()
    for copy in gather_copies + full_copies + seq_copies + reduce_copies:
        copy.wait_send()
    input_grad_out.wait()
    for out in outs:
        out.wait()


def whole_block(layout, modulation, gains, condition, residual, query, key, value, residual_grad, mod_grad):
    rows, width = residual.shape
    local = width // N_SEQ
    heads = local // HEAD_DIM
    tokens = rows * N_SEQ
    n_z, n_y, n_x = layout
    dp_count = n_z + n_y + n_x - 3
    token = VMEM((rows, width), BF16)
    by_head = VMEM((heads, tokens, HEAD_DIM), BF16)

    def stage_bufs():
        return [VMEM((max(n - 1, 1), 8, local), F32) for n in layout]

    hbm = pl.BlockSpec(memory_space=pl.ANY)
    vmem = pl.BlockSpec(memory_space=VMEM)
    big = jax.ShapeDtypeStruct((rows, width), BF16)
    hops = N_SEQ - 1
    return pl.pallas_call(
        functools.partial(kernel, layout),
        out_shape=(big, big, big, big, jax.ShapeDtypeStruct((8, local), F32)),
        in_specs=[vmem] * 3 + [hbm] * 6,
        out_specs=(hbm, hbm, hbm, hbm, vmem),
        scratch_shapes=[
            token,
            token,
            token,
            token,
            token,
            token,
            token,
            token,
            token,
            token,
            VMEM((2, BLOCK, HEAD_DIM), F32),
            VMEM((2, 8, BLOCK), F32),
            VMEM((hops, rows, local), BF16),
            VMEM((hops, rows, local), BF16),
            VMEM((rows, local), F32),
            VMEM((rows, local), F32),
            VMEM((2, width), F32),
            by_head,
            by_head,
            by_head,
            VMEM((N_SEQ, 2, 8, BLOCK), F32),
            VMEM((2, tokens, HEAD_DIM), F32),
            by_head,
            by_head,
            VMEM((heads, tokens, tokens), F32),
            by_head,
            by_head,
            by_head,
            by_head,
            by_head,
            VMEM((tokens, HEAD_DIM), F32),
            VMEM((tokens, HEAD_DIM), F32),
            VMEM((tokens, HEAD_DIM), F32),
            VMEM((8, local), F32),
            VMEM((8, local), F32),
            *stage_bufs(),
            VMEM((3, 8, local), F32),
            VMEM((N_SEQ, 8, local), F32),
            *stage_bufs(),
            VMEM((3, 8, local), F32),
            VMEM((3, 8, width), F32),
            VMEM((8, width), F32),
            VMEM((hops, 8, local), F32),
            DMA((5,)),
            DMA((3, heads)),
            DMA((3, heads, hops)),
            DMA((3, heads, hops)),
            DMA((hops,)),
            DMA((hops,)),
            DMA((heads, hops)),
            DMA((heads, hops)),
            DMA((len(PARTS), heads, hops)),
            DMA((len(PARTS), heads, hops)),
            DMA((3, heads, hops)),
            DMA((3, heads, hops)),
            DMA((dp_count + hops,)),
            DMA((dp_count + hops,)),
            DMA((dp_count + hops,)),
            DMA((dp_count + hops,)),
            DMA((3,)),
            DMA((heads,)),
        ],
        compiler_params=pltpu.CompilerParams(
            collective_id=0, has_side_effects=True, vmem_limit_bytes=58 << 20
        ),
    )(modulation, gains, condition, residual, query, key, value, residual_grad, mod_grad)


def results_kernel(factor, *refs):
    sources, sums_ref, targets, params_ref = refs[:4], refs[4], refs[5:9], refs[9]
    held, in_sem, out_sem = refs[10:]
    count = sources[0].shape[0] // SPLIT
    pieces = [(i, pl.ds(j * count, count), i * SPLIT + j) for i in range(4) for j in range(SPLIT)]
    loads = [
        pltpu.make_async_copy(sources[i].at[at, :], held.at[i, at, :], in_sem.at[n])
        for i, at, n in pieces
    ]
    stores = [
        pltpu.make_async_copy(held.at[i, at, :], targets[i].at[at, :], out_sem.at[n])
        for i, at, n in pieces
    ]
    for load in loads:
        load.start()
    rows, own = params_ref.shape
    params_ref[...] = sums_ref[0:rows, 0:own] * factor
    for load, store in zip(loads, stores):
        load.wait()
        store.start()
    for store in stores:
        store.wait()


def results(factor, own, parts):
    hbm = pl.BlockSpec(memory_space=pl.ANY)
    vmem = pl.BlockSpec(memory_space=VMEM)
    big = [jax.ShapeDtypeStruct(part.shape, part.dtype) for part in parts[:4]]
    return pl.pallas_call(
        functools.partial(results_kernel, factor),
        out_shape=(*big, jax.ShapeDtypeStruct((5, own), F32)),
        in_specs=[hbm] * 4 + [vmem],
        out_specs=(*([hbm] * 4), vmem),
        scratch_shapes=[VMEM((4, *parts[0].shape), BF16), DMA((4 * SPLIT,)), DMA((4 * SPLIT,))],
    )(*parts)


def per_device(
    layout,
    residual,
    query_raw,
    key_raw,
    values,
    residual_grad,
    modulated_grad,
    condition,
    modulation,
    norm_gains,
):
    factor = (residual.shape[0] * lax.axis_size("seq") * lax.axis_size("dp")) ** (-0.5)
    return results(
        factor,
        modulation.shape[1],
        whole_block(
            layout,
            modulation,
            norm_gains,
            condition[0],
            residual,
            query_raw,
            key_raw,
            values,
            residual_grad,
            modulated_grad,
        ),
    )


def solution(mesh):
    layout = (8, 4, mesh.shape["dp"] // 32) if mesh.shape["dp"] >= 32 else (mesh.shape["dp"], 1, 1)
    rows = P(("seq", "dp"), None)
    columns = P(None, ("seq", "dp"))
    return jax.shard_map(
        functools.partial(per_device, layout),
        mesh=mesh,
        in_specs=(rows,) * 6 + (P("dp", None, None), columns, columns),
        out_specs=(rows,) * 4 + (columns,),
        check_vma=False,
    )
```

```python
import functools

import jax
import jax.numpy as jnp
from jax import lax
from jax.experimental import pallas as pl
from jax.experimental.pallas import tpu as pltpu
from jax.sharding import PartitionSpec as P

HEAD_DIM = 128
N_SEQ = 4
EPSILON = 1e-06
SCORE_SCALE = HEAD_DIM ** (-0.5)
MESH = pl.DeviceIdType.MESH
VMEM = pltpu.VMEM
DMA = pltpu.SemaphoreType.DMA
F32 = jnp.float32
BF16 = jnp.bfloat16
BLOCK = 256
CHUNK = 16
PARTS = ((0, 48), (48, 48), (96, 96))
EARLY = 2
SPLIT = 2


def dot_nt(a, b):
    return lax.dot_general(a, b, (((1,), (1,)), ((), ())), preferred_element_type=F32)


def dot_nn(a, b):
    return lax.dot_general(a, b, (((1,), (0,)), ((), ())), preferred_element_type=F32)


def times(start, width):
    return pl.ds(pl.multiple_of(start, width), width)


def kernel(
    layout,
    modulation_ref,
    gains_ref,
    condition_ref,
    residual_hbm,
    query_hbm,
    key_hbm,
    value_hbm,
    residual_grad_hbm,
    modulated_grad_hbm,
    input_grad_hbm,
    query_grad_hbm,
    key_grad_hbm,
    value_grad_hbm,
    sums_ref,
    residual_t,
    query_t,
    key_t,
    residual_grad_t,
    modulated_grad_t,
    attended_t,
    attended_grad_t,
    input_grad_t,
    query_out_t,
    key_out_t,
    scale_t,
    scale_out,
    query_back,
    key_back,
    query_own,
    key_own,
    modulated,
    query_h,
    key_h,
    value_h,
    scale_in,
    scale_h,
    query_n,
    key_n,
    weights_h,
    attended_h,
    grad_h,
    query_grad_h,
    key_grad_h,
    value_grad_h,
    query_total,
    key_total,
    value_total,
    gain_sums,
    gather_z,
    gather_y,
    gather_x,
    got_z,
    got_y,
    got_x,
    mine,
    full,
    reduce_x,
    reduce_y,
    reduce_z,
    back_x,
    back_y,
    back_z,
    total_x,
    total_y,
    columns,
    column_rows,
    seq_parts,
    in_sem,
    own_sem,
    raw_send,
    raw_recv,
    scale_send,
    scale_recv,
    att_send,
    att_recv,
    grad_send,
    grad_recv,
    back_send,
    back_recv,
    gather_send,
    gather_recv,
    reduce_send,
    reduce_recv,
    out_sem,
    value_sem,
):
    n_z, n_y, n_x = layout
    stages = (("z", n_z - 1), ("y", n_y - 1), ("x", n_x - 1))
    dp_count = sum(count for _, count in stages)
    own = modulation_ref.shape[1]
    rows, width = residual_t.shape
    heads = query_h.shape[0]
    local = heads * HEAD_DIM
    tokens = query_h.shape[1]
    s = lax.axis_index("seq")
    d = lax.axis_index("dp")
    hops = range(1, N_SEQ)
    at_z, at_y, at_x = d % n_z, (d // n_z) % n_y, d // (n_z * n_y)
    block_y, block_x = own * n_z, own * n_z * n_y

    def peer(k):
        return (s + k) % N_SEQ

    def sender(k):
        return (s + N_SEQ - k) % N_SEQ

    def dp_partner(stage, k):
        if stage == "z":
            return (d // n_z) * n_z + (d % n_z + k) % n_z
        if stage == "y":
            row = (d // n_z) % n_y
            return d + ((row + k) % n_y - row) * n_z
        return (d + n_z * n_y * k) % (n_z * n_y * n_x)

    def send(src, dst, send_sem, recv_sem, device):
        return pltpu.make_async_remote_copy(
            src_ref=src,
            dst_ref=dst,
            send_sem=send_sem,
            recv_sem=recv_sem,
            device_id=device,
            device_id_type=MESH,
        )

    def head_columns(owner, h):
        return times((owner * heads + h) * HEAD_DIM, HEAD_DIM)

    def token_rows(owner):
        return times(owner * rows, rows)

    raw_hbm = (key_hbm, query_hbm, value_hbm)
    raw_heads = (key_h, query_h, value_h)

    def raw_copy(t, h, k):
        return send(
            raw_hbm[t].at[:, head_columns(peer(k), h)],
            raw_heads[t].at[h, token_rows(s), :],
            raw_send.at[t, h, k - 1],
            raw_recv.at[t, h, k - 1],
            {"seq": peer(k)},
        )

    def own_copy(t, h):
        return pltpu.make_async_copy(
            raw_hbm[t].at[:, head_columns(s, h)],
            raw_heads[t].at[h, token_rows(s), :],
            own_sem.at[t, h],
        )

    def scale_copy(k):
        return send(
            scale_out,
            scale_in.at[s],
            scale_send.at[k - 1],
            scale_recv.at[k - 1],
            {"seq": peer(k)},
        )

    def att_copy(h, k):
        return send(
            attended_h.at[h, token_rows(peer(k)), :],
            attended_t.at[:, head_columns(s, h)],
            att_send.at[h, k - 1],
            att_recv.at[h, k - 1],
            {"seq": peer(k)},
        )

    def part_rows(part):
        first, count = PARTS[part]
        return pl.ds(pl.multiple_of(s * rows + first, CHUNK), count)

    def grad_copy(part, h, k):
        first, count = PARTS[part]
        return send(
            attended_grad_t.at[pl.ds(first, count), head_columns(peer(k), h)],
            grad_h.at[h, part_rows(part), :],
            grad_send.at[part, h, k - 1],
            grad_recv.at[part, h, k - 1],
            {"seq": peer(k)},
        )

    def back_copy(t, h, k):
        if t == 2:
            src, dst = value_grad_h, value_grad_hbm.at[:, head_columns(s, h)]
        else:
            src = (query_grad_h, key_grad_h)[t]
            dst = (query_back, key_back)[t].at[k - 1, :, times(h * HEAD_DIM, HEAD_DIM)]
        return send(
            src.at[h, token_rows(peer(k)), :],
            dst,
            back_send.at[t, h, k - 1],
            back_recv.at[t, h, k - 1],
            {"seq": peer(k)},
        )

    def value_copy(h):
        return pltpu.make_async_copy(
            value_grad_h.at[h, token_rows(s), :],
            value_grad_hbm.at[:, head_columns(s, h)],
            value_sem.at[h],
        )

    def start_raw(h):
        for t in range(3):
            for k in hops:
                raw_copy(t, h, k).start()

    def exchange(stage, sources, targets, send_sem, recv_sem, base):
        copies = [
            send(
                source,
                targets.at[k],
                send_sem.at[base + k],
                recv_sem.at[base + k],
                {"dp": dp_partner(stage, k + 1)},
            )
            for k, source in enumerate(sources)
        ]
        for copy in copies:
            copy.start()
        return copies

    def arrived(start, copies, targets):
        total = start
        for k, copy in enumerate(copies):
            copy.wait_recv()
            total = total + targets[k]
        return total

    def widened(ref, values, shift):
        ref[...] = jnp.zeros_like(ref)
        ref[:, 0 : values.shape[1]] = values
        ref[...] = pltpu.roll(ref[...], shift, 1)

    def window(values, first, count):
        lanes = values.shape[1]
        return pltpu.roll(values, (lanes - first) % lanes, 1)[:, 0:count]

    def start_back(t, h):
        for k in hops:
            back_copy(t, h, k).start()

    inputs = (
        (key_hbm, key_t),
        (query_hbm, query_t),
        (residual_hbm, residual_t),
        (residual_grad_hbm, residual_grad_t),
        (modulated_grad_hbm, modulated_grad_t),
    )
    loads = [
        pltpu.make_async_copy(src, dst, in_sem.at[i]) for i, (src, dst) in enumerate(inputs)
    ]
    for load in loads:
        load.start()
    for t in range(3):
        for h in range(heads):
            own_copy(t, h).start()

    gather_z[...] = jnp.zeros_like(gather_z)
    gather_z[0:2, 0:own] = modulation_ref[...]
    gather_z[2:4, 0:own] = gains_ref[...]
    gather_z[...] = pltpu.roll(gather_z[...], at_z * own, 1)

    partners = [{"seq": peer(k)} for k in hops]
    for stage, count in stages:
        partners += [{"dp": dp_partner(stage, k)} for k in range(1, count + 1)]
    barrier = pltpu.get_barrier_semaphore()
    for partner in partners:
        pl.semaphore_signal(barrier, inc=1, device_id=partner, device_id_type=MESH)
    pl.semaphore_wait(barrier, len(partners))

    def scales():
        scale_t[:, rows:, :] = jnp.zeros((2, BLOCK - rows, HEAD_DIM), F32)
        scale_out[...] = jnp.zeros_like(scale_out)
        for t, source in ((0, key_t), (1, query_t)):
            loads[t].wait()

            @pl.loop(0, rows // CHUNK)
            def _(i):
                at = times(i * CHUNK, CHUNK)
                floats = source[at, :].astype(F32)
                mean = jnp.sum(floats * floats, axis=1, keepdims=True) * (1.0 / width)
                scale_t[t, at, :] = jnp.broadcast_to(
                    lax.rsqrt(mean + EPSILON), (CHUNK, HEAD_DIM)
                )

            scale_out[t : t + 1, :] = scale_t[t].T[0:1, :]
        for k in hops:
            scale_copy(k).start()
        scale_in[s] = scale_out[...]

    copies_z = exchange(
        "z", [gather_z] * (n_z - 1), got_z, gather_send, gather_recv, 0
    )
    start_raw(0)
    scales()
    widened(gather_y, arrived(gather_z[...], copies_z, got_z), at_y * block_y)
    copies_y = exchange(
        "y", [gather_y] * (n_y - 1), got_y, gather_send, gather_recv, n_z - 1
    )
    start_raw(1)
    widened(gather_x, arrived(gather_y[...], copies_y, got_y), at_x * block_x)
    copies_x = exchange(
        "x", [gather_x] * (n_x - 1), got_x, gather_send, gather_recv, n_z + n_y - 2
    )
    start_raw(2)
    mine[...] = arrived(gather_x[...], copies_x, got_x)
    gather_copies = copies_z + copies_y + copies_x
    full[s] = mine[0:4, :]
    full_copies = [
        send(
            mine.at[0:4, :],
            full.at[s],
            gather_send.at[dp_count + k - 1],
            gather_recv.at[dp_count + k - 1],
            {"seq": peer(k)},
        )
        for k in hops
    ]
    for copy in full_copies:
        copy.start()
    for h in range(3, heads):
        start_raw(h)

    for k in hops:
        scale_copy(k).wait_recv()
    for owner in range(N_SEQ):
        for t in range(2):
            spread = jnp.broadcast_to(scale_in[owner, t : t + 1, :], (HEAD_DIM, BLOCK)).T
            scale_h[t, owner * rows : (owner + 1) * rows, :] = spread[0:rows, :]

    @pl.loop(0, heads)
    def _(h):
        gain_at = times(h * HEAD_DIM, HEAD_DIM)
        for t in range(3):
            own_copy(t, h).wait()
            for k in hops:
                raw_copy(t, h, k).wait_recv()
        query_n[h] = (query_h[h].astype(F32) * scale_h[1] * mine[2:3, gain_at]).astype(BF16)
        key_n[h] = (key_h[h].astype(F32) * scale_h[0] * mine[3:4, gain_at]).astype(BF16)
        values_t = value_h[h].T

        @pl.loop(0, tokens // BLOCK)
        def _(i):
            at = times(i * BLOCK, BLOCK)
            scores = dot_nt(key_n[h], query_n[h, at, :]) * SCORE_SCALE
            top = jnp.max(scores, axis=0, keepdims=True)
            raised = jnp.exp(scores - top)
            total = jnp.sum(raised, axis=0, keepdims=True)
            weights = raised * (1.0 / total)
            weights_h[h, :, at] = weights
            attended_h[h, at, :] = dot_nn(values_t, weights.astype(BF16)).T.astype(BF16)

        for k in hops:
            att_copy(h, k).start()
        attended_t[:, head_columns(s, h)] = attended_h[h, token_rows(s), :]

    for copy in full_copies:
        copy.wait_recv()
    for part in range(N_SEQ):
        at = slice(part * local, (part + 1) * local)
        modulated[:, at] = full[part, 0:2, :] + condition_ref[:, at]
    for load in loads[2:]:
        load.wait()
    columns[...] = jnp.zeros_like(columns)

    @pl.loop(0, heads)
    def _(h):
        for k in hops:
            att_copy(h, k).wait_recv()

    for part, (first, count) in enumerate(PARTS):

        @pl.loop(first // CHUNK, (first + count) // CHUNK)
        def _(i):
            at = times(i * CHUNK, CHUNK)
            gate_row = modulated[0:1, :]
            attended = attended_t[at, :].astype(F32)
            summed = residual_t[at, :].astype(F32) + gate_row * attended
            centered = summed - jnp.sum(summed, axis=1, keepdims=True) * (1.0 / width)
            norm_scale = lax.rsqrt(
                jnp.sum(centered * centered, axis=1, keepdims=True) * (1.0 / width) + EPSILON
            )
            normed = centered * norm_scale
            upstream = modulated_grad_t[at, :].astype(F32)
            scaled = upstream * (1.0 + modulated[1:2, :])
            stream_grad = residual_grad_t[at, :].astype(F32) + norm_scale * (
                scaled
                - jnp.sum(scaled, axis=1, keepdims=True) * (1.0 / width)
                - normed * (jnp.sum(scaled * normed, axis=1, keepdims=True) * (1.0 / width))
            )
            input_grad_t[at, :] = stream_grad.astype(BF16)
            attended_grad_t[at, :] = (stream_grad * gate_row).astype(BF16)
            for row, term in enumerate((stream_grad * attended, upstream, upstream * normed)):
                columns[row] += term[0:8, :] + term[8:16, :]

        @pl.loop(0, heads)
        def _(h):
            for k in hops:
                grad_copy(part, h, k).start()
            grad_h[h, part_rows(part), :] = attended_grad_t[
                first : first + count, head_columns(s, h)
            ]

    input_grad_out = pltpu.make_async_copy(input_grad_t, input_grad_hbm, out_sem.at[0])
    input_grad_out.start()
    column_rows[3:8, :] = jnp.zeros((5, width), F32)
    for row in range(3):
        column_rows[row : row + 1, :] = jnp.sum(columns[row], axis=0, keepdims=True)
    seq_copies = [
        send(
            column_rows.at[0:4, times(peer(k) * local, HEAD_DIM * heads)],
            seq_parts.at[k - 1],
            reduce_send.at[dp_count + k - 1],
            reduce_recv.at[dp_count + k - 1],
            {"seq": peer(k)},
        )
        for k in hops
    ]
    for copy in seq_copies:
        copy.start()
    gain_sums[0:3, :] = column_rows[0:3, times(s * local, HEAD_DIM * heads)]
    gain_sums[5:8, :] = jnp.zeros((3, local), F32)

    @pl.loop(0, heads)
    def _(h):
        for part in range(len(PARTS)):
            for k in hops:
                grad_copy(part, h, k).wait_recv()
        at_head = times(h * HEAD_DIM, HEAD_DIM)
        keys_t = key_n[h].T
        key_total[...] = jnp.zeros_like(key_total)
        value_total[...] = jnp.zeros_like(value_total)
        gain_sums[3:4, at_head] = jnp.zeros((1, HEAD_DIM), F32)

        @pl.loop(0, tokens // BLOCK)
        def _(i):
            at = times(i * BLOCK, BLOCK)
            queries = query_n[h, at, :]
            grads = grad_h[h, at, :]
            weights = weights_h[h, :, at]
            product = grads.astype(F32) * attended_h[h, at, :].astype(F32)
            row_dot = jnp.sum(product.T, axis=0, keepdims=True)
            weight_grad = dot_nt(value_h[h], grads)
            score_grad = (weights * (weight_grad - row_dot) * SCORE_SCALE).astype(BF16)
            value_total[...] += dot_nn(weights.astype(BF16), grads)
            key_total[...] += dot_nn(score_grad, queries)
            query_grad = dot_nn(keys_t, score_grad).T
            query_total[at, :] = query_grad
            query_grad_h[h, at, :] = query_grad.astype(BF16)
            gain_sums[3:4, at_head] += jnp.sum(
                query_grad * (query_h[h, at, :].astype(F32) * scale_h[1, at, :]),
                axis=0,
                keepdims=True,
            )

        key_grad_h[h] = key_total[...].astype(BF16)
        value_grad_h[h] = value_total[...].astype(BF16)
        gain_sums[4:5, at_head] = jnp.sum(
            key_total[...] * (key_h[h].astype(F32) * scale_h[0]), axis=0, keepdims=True
        )

        @pl.when(h < EARLY)
        def _():
            for t in range(3):
                start_back(t, h)

        value_copy(h).start()
        query_own[:, at_head] = query_total[token_rows(s), :]
        key_own[:, at_head] = key_total[token_rows(s), :]

    late = [(t, h) for h in range(EARLY, heads) for t in range(2)]
    late += [(2, h) for h in range(EARLY, heads)]

    def start_late(index):
        per_stage = len(late) // 3
        for t, h in late[index * per_stage : (index + 1) * per_stage]:
            start_back(t, h)

    for k, copy in enumerate(seq_copies):
        copy.wait_recv()
        gain_sums[0:3, :] += seq_parts[k, 0:3, :]
    sums = gain_sums[...]
    for k in range(1, n_x):
        reduce_x[k - 1] = window(sums, (at_x + k) % n_x * block_x, reduce_x.shape[2])
    copies_x = exchange(
        "x", [reduce_x.at[k] for k in range(n_x - 1)], back_x, reduce_send, reduce_recv, 0
    )
    start_late(0)
    total_x[...] = arrived(window(sums, at_x * block_x, total_x.shape[1]), copies_x, back_x)
    sums = total_x[...]
    for k in range(1, n_y):
        reduce_y[k - 1] = window(sums, (at_y + k) % n_y * block_y, reduce_y.shape[2])
    copies_y = exchange(
        "y", [reduce_y.at[k] for k in range(n_y - 1)], back_y, reduce_send, reduce_recv, n_x - 1
    )
    start_late(1)
    total_y[...] = arrived(window(sums, at_y * block_y, total_y.shape[1]), copies_y, back_y)
    sums = total_y[...]
    for k in range(1, n_z):
        reduce_z[k - 1] = window(sums, (at_z + k) % n_z * own, reduce_z.shape[2])
    copies_z = exchange(
        "z",
        [reduce_z.at[k] for k in range(n_z - 1)],
        back_z,
        reduce_send,
        reduce_recv,
        n_x + n_y - 2,
    )
    start_late(2)
    sums_ref[...] = arrived(window(sums, at_z * own, sums_ref.shape[1]), copies_z, back_z)
    reduce_copies = copies_x + copies_y + copies_z

    outs = []
    for t, (raw, back, own, out, out_hbm, scale_row, gain_row) in enumerate(
        (
            (query_t, query_back, query_own, query_out_t, query_grad_hbm, 1, 2),
            (key_t, key_back, key_own, key_out_t, key_grad_hbm, 0, 3),
        )
    ):

        @pl.loop(0, heads)
        def _(h):
            for k in hops:
                back_copy(t, h, k).wait_recv()

        @pl.loop(0, rows // CHUNK)
        def _(i):
            at = times(i * CHUNK, CHUNK)
            inverse = scale_t[scale_row, at, 0:1]
            parts = []
            mean = jnp.zeros((CHUNK, 1), F32)
            for k in range(N_SEQ):
                block = sender(k)
                where = times(block * local, HEAD_DIM * heads)
                upstream = own[at, :] if k == 0 else back[k - 1, at, :].astype(F32)
                weighted = full[block, gain_row : gain_row + 1, :] * upstream
                floats = raw[at, where].astype(F32)
                mean = mean + jnp.sum(floats * weighted, axis=1, keepdims=True)
                parts.append((where, weighted, floats))
            factor = inverse * inverse * inverse * (mean * (1.0 / width))
            for where, weighted, floats in parts:
                out[at, where] = (inverse * weighted - floats * factor).astype(BF16)

        outs.append(pltpu.make_async_copy(out, out_hbm, out_sem.at[1 + t]))
        outs[-1].start()

    @pl.loop(0, heads)
    def _(h):
        for t in range(3):
            for k in hops:
                raw_copy(t, h, k).wait_send()
                back_copy(t, h, k).wait_send()
        for k in hops:
            back_copy(2, h, k).wait_recv()
            att_copy(h, k).wait_send()
            for part in range(len(PARTS)):
                grad_copy(part, h, k).wait_send()
        value_copy(h).wait()

    for k in hops:
        scale_copy(k).wait_send()
    for copy in gather_copies + full_copies + seq_copies + reduce_copies:
        copy.wait_send()
    input_grad_out.wait()
    for out in outs:
        out.wait()


def whole_block(layout, modulation, gains, condition, residual, query, key, value, residual_grad, mod_grad):
    rows, width = residual.shape
    local = width // N_SEQ
    heads = local // HEAD_DIM
    tokens = rows * N_SEQ
    n_z, n_y, n_x = layout
    dp_count = n_z + n_y + n_x - 3
    token = VMEM((rows, width), BF16)
    by_head = VMEM((heads, tokens, HEAD_DIM), BF16)

    own = modulation.shape[1]
    wide_own, wide_z, wide_y = (
        -(-lanes // HEAD_DIM) * HEAD_DIM for lanes in (own, own * n_z, own * n_z * n_y)
    )
    hbm = pl.BlockSpec(memory_space=pl.ANY)
    vmem = pl.BlockSpec(memory_space=VMEM)
    big = jax.ShapeDtypeStruct((rows, width), BF16)
    hops = N_SEQ - 1
    return pl.pallas_call(
        functools.partial(kernel, layout),
        out_shape=(big, big, big, big, jax.ShapeDtypeStruct((8, wide_own), F32)),
        in_specs=[vmem] * 3 + [pl.BlockSpec(memory_space=pltpu.HBM)] * 6,
        out_specs=(hbm, hbm, hbm, hbm, vmem),
        scratch_shapes=[
            token,
            token,
            token,
            token,
            token,
            token,
            token,
            token,
            token,
            token,
            VMEM((2, BLOCK, HEAD_DIM), F32),
            VMEM((8, BLOCK), F32),
            VMEM((hops, rows, local), BF16),
            VMEM((hops, rows, local), BF16),
            VMEM((rows, local), F32),
            VMEM((rows, local), F32),
            VMEM((2, width), F32),
            by_head,
            by_head,
            by_head,
            VMEM((N_SEQ, 8, BLOCK), F32),
            VMEM((2, tokens, HEAD_DIM), F32),
            by_head,
            by_head,
            VMEM((heads, tokens, tokens), F32),
            by_head,
            by_head,
            by_head,
            by_head,
            by_head,
            VMEM((tokens, HEAD_DIM), F32),
            VMEM((tokens, HEAD_DIM), F32),
            VMEM((tokens, HEAD_DIM), F32),
            VMEM((8, local), F32),
            VMEM((8, wide_z), F32),
            VMEM((8, wide_y), F32),
            VMEM((8, local), F32),
            VMEM((max(n_z - 1, 1), 8, wide_z), F32),
            VMEM((max(n_y - 1, 1), 8, wide_y), F32),
            VMEM((max(n_x - 1, 1), 8, local), F32),
            VMEM((8, local), F32),
            VMEM((N_SEQ, 4, local), F32),
            VMEM((max(n_x - 1, 1), 8, wide_y), F32),
            VMEM((max(n_y - 1, 1), 8, wide_z), F32),
            VMEM((max(n_z - 1, 1), 8, wide_own), F32),
            VMEM((max(n_x - 1, 1), 8, wide_y), F32),
            VMEM((max(n_y - 1, 1), 8, wide_z), F32),
            VMEM((max(n_z - 1, 1), 8, wide_own), F32),
            VMEM((8, wide_y), F32),
            VMEM((8, wide_z), F32),
            VMEM((3, 8, width), F32),
            VMEM((8, width), F32),
            VMEM((hops, 4, local), F32),
            DMA((5,)),
            DMA((3, heads)),
            DMA((3, heads, hops)),
            DMA((3, heads, hops)),
            DMA((hops,)),
            DMA((hops,)),
            DMA((heads, hops)),
            DMA((heads, hops)),
            DMA((len(PARTS), heads, hops)),
            DMA((len(PARTS), heads, hops)),
            DMA((3, heads, hops)),
            DMA((3, heads, hops)),
            DMA((dp_count + hops,)),
            DMA((dp_count + hops,)),
            DMA((dp_count + hops,)),
            DMA((dp_count + hops,)),
            DMA((3,)),
            DMA((heads,)),
        ],
        compiler_params=pltpu.CompilerParams(
            collective_id=0, has_side_effects=True, vmem_limit_bytes=44 << 20
        ),
    )(modulation, gains, condition, residual, query, key, value, residual_grad, mod_grad)


def results_kernel(factor, *refs):
    sources, sums_ref, targets, params_ref, sem = refs[:4], refs[4], refs[5:9], refs[9], refs[10]
    copies = [
        pltpu.make_async_copy(source, target, sem.at[i])
        for i, (source, target) in enumerate(zip(sources, targets))
    ]
    for copy in copies:
        copy.start()
    rows, own = params_ref.shape
    params_ref[...] = sums_ref[0:rows, 0:own] * factor
    for copy in copies:
        copy.wait()


def results(factor, own, parts):
    hbm = pl.BlockSpec(memory_space=pltpu.HBM)
    vmem = pl.BlockSpec(memory_space=VMEM)
    big = [jax.ShapeDtypeStruct(part.shape, part.dtype) for part in parts[:4]]
    return pl.pallas_call(
        functools.partial(results_kernel, factor),
        out_shape=(*big, jax.ShapeDtypeStruct((5, own), F32)),
        in_specs=[vmem] * 4 + [vmem],
        out_specs=(*([hbm] * 4), vmem),
        scratch_shapes=[DMA((4,))],
        compiler_params=pltpu.CompilerParams(vmem_limit_bytes=8 << 20),
    )(*parts)


def per_device(
    layout,
    residual,
    query_raw,
    key_raw,
    values,
    residual_grad,
    modulated_grad,
    condition,
    modulation,
    norm_gains,
):
    residual, query_raw, key_raw, values, residual_grad, modulated_grad = (
        pltpu.with_memory_space_constraint(x, pltpu.HBM)
        for x in (residual, query_raw, key_raw, values, residual_grad, modulated_grad)
    )
    condition, modulation, norm_gains = (
        pltpu.with_memory_space_constraint(x, pltpu.HBM)
        for x in (condition[0], modulation, norm_gains)
    )
    factor = (residual.shape[0] * lax.axis_size("seq") * lax.axis_size("dp")) ** (-0.5)
    return results(
        factor,
        modulation.shape[1],
        whole_block(
            layout,
            modulation,
            norm_gains,
            condition,
            residual,
            query_raw,
            key_raw,
            values,
            residual_grad,
            modulated_grad,
        ),
    )


def solution(mesh):
    layout = (8, 4, mesh.shape["dp"] // 32) if mesh.shape["dp"] >= 32 else (mesh.shape["dp"], 1, 1)
    rows = P(("seq", "dp"), None)
    columns = P(None, ("seq", "dp"))
    return jax.shard_map(
        functools.partial(per_device, layout),
        mesh=mesh,
        in_specs=(rows,) * 6 + (P("dp", None, None), columns, columns),
        out_specs=(rows,) * 4 + (columns,),
        check_vma=False,
    )
```

```python
import functools

import jax
import jax.numpy as jnp
from jax import lax
from jax.experimental import pallas as pl
from jax.experimental.pallas import tpu as pltpu
from jax.sharding import PartitionSpec as P

HEAD_DIM = 128
N_SEQ = 4
EPSILON = 1e-06
SCORE_SCALE = HEAD_DIM ** (-0.5)
MESH = pl.DeviceIdType.MESH
VMEM = pltpu.VMEM
DMA = pltpu.SemaphoreType.DMA
F32 = jnp.float32
BF16 = jnp.bfloat16
BLOCK = 256
CHUNK = 16
HALVES = 2
EARLY = 2
SPLIT = 2


def dot_nt(a, b):
    return lax.dot_general(a, b, (((1,), (1,)), ((), ())), preferred_element_type=F32)


def dot_nn(a, b):
    return lax.dot_general(a, b, (((1,), (0,)), ((), ())), preferred_element_type=F32)


def times(start, width):
    return pl.ds(pl.multiple_of(start, width), width)


def kernel(
    layout,
    modulation_ref,
    gains_ref,
    condition_ref,
    residual_hbm,
    query_hbm,
    key_hbm,
    value_hbm,
    residual_grad_hbm,
    modulated_grad_hbm,
    input_grad_hbm,
    query_grad_hbm,
    key_grad_hbm,
    value_grad_hbm,
    sums_ref,
    residual_t,
    query_t,
    key_t,
    residual_grad_t,
    modulated_grad_t,
    attended_t,
    attended_grad_t,
    input_grad_t,
    query_out_t,
    key_out_t,
    scale_t,
    scale_out,
    query_back,
    key_back,
    query_own,
    key_own,
    modulated,
    query_h,
    key_h,
    value_h,
    scale_in,
    scale_h,
    query_n,
    key_n,
    weights_h,
    attended_h,
    grad_h,
    query_grad_h,
    key_grad_h,
    value_grad_h,
    query_total,
    key_total,
    value_total,
    gain_sums,
    gather_z,
    gather_y,
    gather_x,
    got_z,
    got_y,
    got_x,
    mine,
    full,
    reduce_x,
    reduce_y,
    reduce_z,
    back_x,
    back_y,
    back_z,
    total_x,
    total_y,
    columns,
    column_rows,
    seq_parts,
    in_sem,
    own_sem,
    raw_send,
    raw_recv,
    scale_send,
    scale_recv,
    att_send,
    att_recv,
    grad_send,
    grad_recv,
    wide_send,
    wide_recv,
    back_send,
    back_recv,
    value_send,
    value_recv,
    gather_send,
    gather_recv,
    reduce_send,
    reduce_recv,
    out_sem,
    value_sem,
):
    n_z, n_y, n_x = layout
    stages = (("z", n_z - 1), ("y", n_y - 1), ("x", n_x - 1))
    dp_count = sum(count for _, count in stages)
    own = modulation_ref.shape[1]
    rows, width = residual_t.shape
    heads = query_h.shape[0]
    local = heads * HEAD_DIM
    tokens = query_h.shape[1]
    s = lax.axis_index("seq")
    d = lax.axis_index("dp")
    hops = range(1, N_SEQ)
    part_size = rows // HALVES
    part_queries = tokens // HALVES
    at_z, at_y, at_x = d % n_z, (d // n_z) % n_y, d // (n_z * n_y)
    block_y, block_x = own * n_z, own * n_z * n_y

    def peer(k):
        return (s + k) % N_SEQ

    def sender(k):
        return (s + N_SEQ - k) % N_SEQ

    def dp_partner(stage, k):
        if stage == "z":
            return (d // n_z) * n_z + (d % n_z + k) % n_z
        if stage == "y":
            row = (d // n_z) % n_y
            return d + ((row + k) % n_y - row) * n_z
        return (d + n_z * n_y * k) % (n_z * n_y * n_x)

    def send(src, dst, send_sem, recv_sem, device):
        return pltpu.make_async_remote_copy(
            src_ref=src,
            dst_ref=dst,
            send_sem=send_sem,
            recv_sem=recv_sem,
            device_id=device,
            device_id_type=MESH,
        )

    def head_columns(owner, h):
        return times((owner * heads + h) * HEAD_DIM, HEAD_DIM)

    def token_rows(owner):
        return times(owner * rows, rows)

    def part_rows(part):
        return pl.ds(part * part_size, part_size)

    def query_rows(part, owner):
        start = part * part_queries + owner * part_size
        return pl.ds(pl.multiple_of(start, part_size), part_size)

    def raw_refs(t, h, owner):
        at = head_columns(owner, h)
        if t in (0, 2):
            source, target = ((key_hbm, key_h), (value_hbm, value_h))[t // 2]
            return source.at[:, at], target.at[h, token_rows(s), :]
        part = t // 2
        return query_hbm.at[part_rows(part), at], query_h.at[h, query_rows(part, s), :]

    def raw_copy(t, h, k):
        return send(
            *raw_refs(t, h, peer(k)),
            raw_send.at[t, h, k - 1],
            raw_recv.at[t, h, k - 1],
            {"seq": peer(k)},
        )

    def own_copy(t, h):
        return pltpu.make_async_copy(*raw_refs(t, h, s), own_sem.at[t, h])

    def scale_copy(k):
        return send(
            scale_out,
            scale_in.at[s],
            scale_send.at[k - 1],
            scale_recv.at[k - 1],
            {"seq": peer(k)},
        )

    def att_copy(part, h, k):
        return send(
            attended_h.at[h, query_rows(part, peer(k)), :],
            attended_t.at[part_rows(part), head_columns(s, h)],
            att_send.at[part, h, k - 1],
            att_recv.at[part, h, k - 1],
            {"seq": peer(k)},
        )

    def grad_copy(part, k):
        return send(
            attended_grad_t.at[part_rows(part), times(peer(k) * local, HEAD_DIM * heads)],
            grad_h.at[query_rows(part, s), :],
            wide_send.at[part, k - 1],
            wide_recv.at[part, k - 1],
            {"seq": peer(k)},
        )

    def last_grad_copy(h, k):
        part = HALVES - 1
        return send(
            attended_grad_t.at[part_rows(part), head_columns(peer(k), h)],
            grad_h.at[query_rows(part, s), times(h * HEAD_DIM, HEAD_DIM)],
            grad_send.at[h, k - 1],
            grad_recv.at[h, k - 1],
            {"seq": peer(k)},
        )

    def back_copy(t, h, k):
        at = times(h * HEAD_DIM, HEAD_DIM)
        if t == 1:
            source = key_grad_h.at[h, token_rows(peer(k)), :]
            target = key_back.at[k - 1, :, at]
        else:
            source = query_grad_h.at[h, query_rows(t // 2, peer(k)), :]
            target = query_back.at[k - 1, part_rows(t // 2), at]
        return send(
            source,
            target,
            back_send.at[t, h, k - 1],
            back_recv.at[t, h, k - 1],
            {"seq": peer(k)},
        )

    def value_back(h, k, count=1):
        return send(
            value_grad_h.at[token_rows(peer(k)), pl.ds(pl.multiple_of(h * HEAD_DIM, HEAD_DIM), count * HEAD_DIM)],
            value_grad_hbm.at[
                :,
                pl.ds(pl.multiple_of((s * heads + h) * HEAD_DIM, HEAD_DIM), count * HEAD_DIM),
            ],
            value_send.at[h, k - 1],
            value_recv.at[h, k - 1],
            {"seq": peer(k)},
        )

    value_own = pltpu.make_async_copy(
        value_grad_h.at[token_rows(s), :],
        value_grad_hbm.at[:, times(s * local, HEAD_DIM * heads)],
        value_sem.at[0],
    )

    def start_raw(h):
        for t in range(3):
            for k in hops:
                raw_copy(t, h, k).start()

    def exchange(stage, sources, targets, send_sem, recv_sem, base):
        copies = [
            send(
                source,
                targets.at[k],
                send_sem.at[base + k],
                recv_sem.at[base + k],
                {"dp": dp_partner(stage, k + 1)},
            )
            for k, source in enumerate(sources)
        ]
        for copy in copies:
            copy.start()
        return copies

    def arrived(start, copies, targets):
        total = start
        for k, copy in enumerate(copies):
            copy.wait_recv()
            total = total + targets[k]
        return total

    def widened(ref, values, shift):
        ref[...] = jnp.zeros_like(ref)
        ref[:, 0 : values.shape[1]] = values
        ref[...] = pltpu.roll(ref[...], shift, 1)

    def window(values, first, count):
        lanes = values.shape[1]
        return pltpu.roll(values, (lanes - first) % lanes, 1)[:, 0:count]

    def start_back(t, h):
        for k in hops:
            back_copy(t, h, k).start()

    inputs = (
        (key_hbm, key_t),
        (query_hbm, query_t),
        (residual_hbm, residual_t),
        (residual_grad_hbm, residual_grad_t),
        (modulated_grad_hbm, modulated_grad_t),
    )
    loads = [
        pltpu.make_async_copy(src, dst, in_sem.at[i]) for i, (src, dst) in enumerate(inputs)
    ]
    partners = [{"seq": peer(k)} for k in hops]
    for stage, count in stages:
        partners += [{"dp": dp_partner(stage, k)} for k in range(1, count + 1)]
    barrier = pltpu.get_barrier_semaphore()
    for partner in partners:
        pl.semaphore_signal(barrier, inc=1, device_id=partner, device_id_type=MESH)
    gather_z[...] = jnp.zeros_like(gather_z)
    gather_z[0:2, 0:own] = modulation_ref[...]
    gather_z[2:4, 0:own] = gains_ref[...]
    gather_z[...] = pltpu.roll(gather_z[...], at_z * own, 1)

    pl.semaphore_wait(barrier, len(partners))

    def scales():
        scale_t[:, rows:, :] = jnp.zeros((2, BLOCK - rows, HEAD_DIM), F32)
        scale_out[...] = jnp.zeros_like(scale_out)
        for t, source in ((0, key_t), (1, query_t)):
            loads[t].wait()

            @pl.loop(0, rows // CHUNK)
            def _(i):
                at = times(i * CHUNK, CHUNK)
                floats = source[at, :].astype(F32)
                mean = jnp.sum(floats * floats, axis=1, keepdims=True) * (1.0 / width)
                scale_t[t, at, :] = jnp.broadcast_to(
                    lax.rsqrt(mean + EPSILON), (CHUNK, HEAD_DIM)
                )

            scale_out[t : t + 1, :] = scale_t[t].T[0:1, :]
        for k in hops:
            scale_copy(k).start()
        scale_in[s] = scale_out[...]

    copies_z = exchange(
        "z", [gather_z] * (n_z - 1), got_z, gather_send, gather_recv, 0
    )
    start_raw(0)
    for load in loads:
        load.start()
    for t in range(4):
        for h in range(heads):
            own_copy(t, h).start()
    scales()
    widened(gather_y, arrived(gather_z[...], copies_z, got_z), at_y * block_y)
    copies_y = exchange(
        "y", [gather_y] * (n_y - 1), got_y, gather_send, gather_recv, n_z - 1
    )
    start_raw(1)
    widened(gather_x, arrived(gather_y[...], copies_y, got_y), at_x * block_x)
    copies_x = exchange(
        "x", [gather_x] * (n_x - 1), got_x, gather_send, gather_recv, n_z + n_y - 2
    )
    start_raw(2)
    mine[...] = arrived(gather_x[...], copies_x, got_x)
    gather_copies = copies_z + copies_y + copies_x
    full[s] = mine[0:4, :]
    full_copies = [
        send(
            mine.at[0:4, :],
            full.at[s],
            gather_send.at[dp_count + k - 1],
            gather_recv.at[dp_count + k - 1],
            {"seq": peer(k)},
        )
        for k in hops
    ]
    for copy in full_copies:
        copy.start()
    for h in range(3, heads):
        start_raw(h)
    for h in range(heads):
        for k in hops:
            raw_copy(3, h, k).start()

    for k in hops:
        scale_copy(k).wait_recv()
    for owner in range(N_SEQ):
        for t in range(2):
            spread = jnp.broadcast_to(scale_in[owner, t : t + 1, :], (HEAD_DIM, BLOCK)).T
            if t == 0:
                scale_h[t, owner * rows : (owner + 1) * rows, :] = spread[0:rows, :]
            else:
                for part in range(HALVES):
                    at = part * part_queries + owner * part_size
                    scale_h[t, at : at + part_size, :] = spread[
                        part * part_size : (part + 1) * part_size, :
                    ]

    for part, sent in ((0, (0, 1, 2)), (1, (3,))):
        at = slice(part * part_queries, (part + 1) * part_queries)

        @pl.loop(0, heads)
        def _(h):
            gain_at = times(h * HEAD_DIM, HEAD_DIM)
            for t in sent:
                own_copy(t, h).wait()
                for k in hops:
                    raw_copy(t, h, k).wait_recv()
            query_n[h, at, :] = (
                query_h[h, at, :].astype(F32) * scale_h[1, at, :] * mine[2:3, gain_at]
            ).astype(BF16)
            if part == 0:
                key_n[h] = (key_h[h].astype(F32) * scale_h[0] * mine[3:4, gain_at]).astype(BF16)
            scores = dot_nt(key_n[h], query_n[h, at, :]) * SCORE_SCALE
            top = jnp.max(scores, axis=0, keepdims=True)
            raised = jnp.exp(scores - top)
            total = jnp.sum(raised, axis=0, keepdims=True)
            weights = raised * (1.0 / total)
            weights_h[h, :, at] = weights
            attended_h[h, at, :] = dot_nn(value_h[h].T, weights.astype(BF16)).T.astype(BF16)
            for k in hops:
                att_copy(part, h, k).start()
            attended_t[part_rows(part), head_columns(s, h)] = attended_h[
                h, query_rows(part, s), :
            ]

    for copy in full_copies:
        copy.wait_recv()
    for part in range(N_SEQ):
        at = slice(part * local, (part + 1) * local)
        modulated[:, at] = full[part, 0:2, :] + condition_ref[:, at]
    for load in loads[2:]:
        load.wait()
    columns[...] = jnp.zeros_like(columns)

    for part in range(HALVES):

        @pl.loop(0, heads)
        def _(h):
            for k in hops:
                att_copy(part, h, k).wait_recv()

        @pl.loop(part * part_size // CHUNK, (part + 1) * part_size // CHUNK)
        def _(i):
            at = times(i * CHUNK, CHUNK)
            gate_row = modulated[0:1, :]
            attended = attended_t[at, :].astype(F32)
            summed = residual_t[at, :].astype(F32) + gate_row * attended
            centered = summed - jnp.sum(summed, axis=1, keepdims=True) * (1.0 / width)
            norm_scale = lax.rsqrt(
                jnp.sum(centered * centered, axis=1, keepdims=True) * (1.0 / width) + EPSILON
            )
            normed = centered * norm_scale
            upstream = modulated_grad_t[at, :].astype(F32)
            scaled = upstream * (1.0 + modulated[1:2, :])
            stream_grad = residual_grad_t[at, :].astype(F32) + norm_scale * (
                scaled
                - jnp.sum(scaled, axis=1, keepdims=True) * (1.0 / width)
                - normed * (jnp.sum(scaled * normed, axis=1, keepdims=True) * (1.0 / width))
            )
            input_grad_t[at, :] = stream_grad.astype(BF16)
            attended_grad_t[at, :] = (stream_grad * gate_row).astype(BF16)
            for row, term in enumerate((stream_grad * attended, upstream, upstream * normed)):
                columns[row] += term[0:8, :] + term[8:16, :]

        if part < HALVES - 1:
            for k in hops:
                grad_copy(part, k).start()
        else:

            @pl.loop(0, heads)
            def _(h):
                for k in hops:
                    last_grad_copy(h, k).start()

        grad_h[query_rows(part, s), :] = attended_grad_t[
            part_rows(part), times(s * local, HEAD_DIM * heads)
        ]

    input_grad_out = pltpu.make_async_copy(input_grad_t, input_grad_hbm, out_sem.at[0])
    input_grad_out.start()
    column_rows[3:8, :] = jnp.zeros((5, width), F32)
    for row in range(3):
        column_rows[row : row + 1, :] = jnp.sum(columns[row], axis=0, keepdims=True)
    seq_copies = [
        send(
            column_rows.at[0:4, times(peer(k) * local, HEAD_DIM * heads)],
            seq_parts.at[k - 1],
            reduce_send.at[dp_count + k - 1],
            reduce_recv.at[dp_count + k - 1],
            {"seq": peer(k)},
        )
        for k in hops
    ]
    for copy in seq_copies:
        copy.start()
    gain_sums[0:3, :] = column_rows[0:3, times(s * local, HEAD_DIM * heads)]
    gain_sums[5:8, :] = jnp.zeros((3, local), F32)

    for part in range(HALVES - 1):
        for k in hops:
            grad_copy(part, k).wait_recv()

    @pl.loop(0, heads)
    def _(h):
        for k in hops:
            last_grad_copy(h, k).wait_recv()
        at_head = times(h * HEAD_DIM, HEAD_DIM)
        keys_t = key_n[h].T
        key_total[...] = jnp.zeros_like(key_total)
        value_total[...] = jnp.zeros_like(value_total)
        gain_sums[3:4, at_head] = jnp.zeros((1, HEAD_DIM), F32)

        @pl.loop(0, tokens // BLOCK)
        def _(i):
            at = times(i * BLOCK, BLOCK)
            queries = query_n[h, at, :]
            grads = grad_h[at, at_head]
            weights = weights_h[h, :, at]
            product = grads.astype(F32) * attended_h[h, at, :].astype(F32)
            row_dot = jnp.sum(product.T, axis=0, keepdims=True)
            weight_grad = dot_nt(value_h[h], grads)
            score_grad = (weights * (weight_grad - row_dot) * SCORE_SCALE).astype(BF16)
            value_total[...] += dot_nn(weights.astype(BF16), grads)
            key_total[...] += dot_nn(score_grad, queries)
            query_grad = dot_nn(keys_t, score_grad).T
            query_total[at, :] = query_grad
            query_grad_h[h, at, :] = query_grad.astype(BF16)
            gain_sums[3:4, at_head] += jnp.sum(
                query_grad * (query_h[h, at, :].astype(F32) * scale_h[1, at, :]),
                axis=0,
                keepdims=True,
            )

        key_grad_h[h] = key_total[...].astype(BF16)
        value_grad_h[:, at_head] = value_total[...].astype(BF16)
        gain_sums[4:5, at_head] = jnp.sum(
            key_total[...] * (key_h[h].astype(F32) * scale_h[0]), axis=0, keepdims=True
        )

        @pl.when(h < EARLY)
        def _():
            for t in range(3):
                start_back(t, h)
            for k in hops:
                value_back(h, k).start()

        for part in range(HALVES):
            query_own[part_rows(part), at_head] = query_total[query_rows(part, s), :]
        key_own[:, at_head] = key_total[token_rows(s), :]

    value_own.start()

    late = [(t, h) for h in range(EARLY, heads) for t in (0, 2, 1)]
    middle = (len(late) + 1) // 2

    def start_late(index):
        for t, h in (late[:middle], late[middle:])[index]:
            start_back(t, h)

    for k, copy in enumerate(seq_copies):
        copy.wait_recv()
        gain_sums[0:3, :] += seq_parts[k, 0:3, :]
    sums = gain_sums[...]
    for k in range(1, n_x):
        reduce_x[k - 1] = window(sums, (at_x + k) % n_x * block_x, reduce_x.shape[2])
    copies_x = exchange(
        "x", [reduce_x.at[k] for k in range(n_x - 1)], back_x, reduce_send, reduce_recv, 0
    )
    start_late(0)
    total_x[...] = arrived(window(sums, at_x * block_x, total_x.shape[1]), copies_x, back_x)
    sums = total_x[...]
    for k in range(1, n_y):
        reduce_y[k - 1] = window(sums, (at_y + k) % n_y * block_y, reduce_y.shape[2])
    copies_y = exchange(
        "y", [reduce_y.at[k] for k in range(n_y - 1)], back_y, reduce_send, reduce_recv, n_x - 1
    )
    start_late(1)
    total_y[...] = arrived(window(sums, at_y * block_y, total_y.shape[1]), copies_y, back_y)
    sums = total_y[...]
    for k in range(1, n_z):
        reduce_z[k - 1] = window(sums, (at_z + k) % n_z * own, reduce_z.shape[2])
    copies_z = exchange(
        "z",
        [reduce_z.at[k] for k in range(n_z - 1)],
        back_z,
        reduce_send,
        reduce_recv,
        n_x + n_y - 2,
    )
    for k in hops:
        value_back(EARLY, k, heads - EARLY).start()
    sums_ref[...] = arrived(window(sums, at_z * own, sums_ref.shape[1]), copies_z, back_z)
    reduce_copies = copies_x + copies_y + copies_z

    @pl.loop(0, heads)
    def _(h):
        for k in hops:
            for t in range(4):
                raw_copy(t, h, k).wait_send()
            for part in range(HALVES):
                att_copy(part, h, k).wait_send()
            last_grad_copy(h, k).wait_send()

    for k in hops:
        scale_copy(k).wait_send()
        for part in range(HALVES - 1):
            grad_copy(part, k).wait_send()
    for copy in gather_copies + full_copies + seq_copies:
        copy.wait_send()

    outs = []
    for t, (raw, back, own, out, out_hbm, scale_row, gain_row) in enumerate(
        (
            (query_t, query_back, query_own, query_out_t, query_grad_hbm, 1, 2),
            (key_t, key_back, key_own, key_out_t, key_grad_hbm, 0, 3),
        )
    ):

        @pl.loop(0, heads)
        def _(h):
            for piece in ((0, 2), (1,))[t]:
                for k in hops:
                    back_copy(piece, h, k).wait_recv()

        @pl.loop(0, rows // CHUNK)
        def _(i):
            at = times(i * CHUNK, CHUNK)
            inverse = scale_t[scale_row, at, 0:1]
            parts = []
            mean = jnp.zeros((CHUNK, 1), F32)
            for k in range(N_SEQ):
                block = sender(k)
                where = times(block * local, HEAD_DIM * heads)
                upstream = own[at, :] if k == 0 else back[k - 1, at, :].astype(F32)
                weighted = full[block, gain_row : gain_row + 1, :] * upstream
                floats = raw[at, where].astype(F32)
                mean = mean + jnp.sum(floats * weighted, axis=1, keepdims=True)
                parts.append((where, weighted, floats))
            factor = inverse * inverse * inverse * (mean * (1.0 / width))
            for where, weighted, floats in parts:
                out[at, where] = (inverse * weighted - floats * factor).astype(BF16)

        outs.append(pltpu.make_async_copy(out, out_hbm, out_sem.at[1 + t]))
        outs[-1].start()

    @pl.loop(0, heads)
    def _(h):
        for t in range(3):
            for k in hops:
                back_copy(t, h, k).wait_send()

    for copy in reduce_copies:
        copy.wait_send()
    value_own.wait()
    for k in hops:
        for h in range(EARLY):
            value_back(h, k).wait()
        value_back(EARLY, k, heads - EARLY).wait()
    input_grad_out.wait()
    for out in outs:
        out.wait()


def whole_block(layout, modulation, gains, condition, residual, query, key, value, residual_grad, mod_grad):
    rows, width = residual.shape
    local = width // N_SEQ
    heads = local // HEAD_DIM
    tokens = rows * N_SEQ
    n_z, n_y, n_x = layout
    dp_count = n_z + n_y + n_x - 3
    token = VMEM((rows, width), BF16)
    by_head = VMEM((heads, tokens, HEAD_DIM), BF16)

    own = modulation.shape[1]
    wide_own, wide_z, wide_y = (
        -(-lanes // HEAD_DIM) * HEAD_DIM for lanes in (own, own * n_z, own * n_z * n_y)
    )
    hbm = pl.BlockSpec(memory_space=pl.ANY)
    vmem = pl.BlockSpec(memory_space=VMEM)
    big = jax.ShapeDtypeStruct((rows, width), BF16)
    hops = N_SEQ - 1
    return pl.pallas_call(
        functools.partial(kernel, layout),
        out_shape=(big, big, big, big, jax.ShapeDtypeStruct((8, wide_own), F32)),
        in_specs=[vmem] * 3 + [pl.BlockSpec(memory_space=pltpu.HBM)] * 6,
        out_specs=(hbm, hbm, hbm, hbm, vmem),
        scratch_shapes=[
            token,
            token,
            token,
            token,
            token,
            token,
            token,
            token,
            token,
            token,
            VMEM((2, BLOCK, HEAD_DIM), F32),
            VMEM((8, BLOCK), F32),
            VMEM((hops, rows, local), BF16),
            VMEM((hops, rows, local), BF16),
            VMEM((rows, local), F32),
            VMEM((rows, local), F32),
            VMEM((2, width), F32),
            by_head,
            by_head,
            by_head,
            VMEM((N_SEQ, 8, BLOCK), F32),
            VMEM((2, tokens, HEAD_DIM), F32),
            by_head,
            by_head,
            VMEM((heads, tokens, tokens), F32),
            by_head,
            VMEM((tokens, local), BF16),
            by_head,
            by_head,
            VMEM((tokens, local), BF16),
            VMEM((tokens, HEAD_DIM), F32),
            VMEM((tokens, HEAD_DIM), F32),
            VMEM((tokens, HEAD_DIM), F32),
            VMEM((8, local), F32),
            VMEM((8, wide_z), F32),
            VMEM((8, wide_y), F32),
            VMEM((8, local), F32),
            VMEM((max(n_z - 1, 1), 8, wide_z), F32),
            VMEM((max(n_y - 1, 1), 8, wide_y), F32),
            VMEM((max(n_x - 1, 1), 8, local), F32),
            VMEM((8, local), F32),
            VMEM((N_SEQ, 4, local), F32),
            VMEM((max(n_x - 1, 1), 8, wide_y), F32),
            VMEM((max(n_y - 1, 1), 8, wide_z), F32),
            VMEM((max(n_z - 1, 1), 8, wide_own), F32),
            VMEM((max(n_x - 1, 1), 8, wide_y), F32),
            VMEM((max(n_y - 1, 1), 8, wide_z), F32),
            VMEM((max(n_z - 1, 1), 8, wide_own), F32),
            VMEM((8, wide_y), F32),
            VMEM((8, wide_z), F32),
            VMEM((3, 8, width), F32),
            VMEM((8, width), F32),
            VMEM((hops, 4, local), F32),
            DMA((5,)),
            DMA((4, heads)),
            DMA((4, heads, hops)),
            DMA((4, heads, hops)),
            DMA((hops,)),
            DMA((hops,)),
            DMA((HALVES, heads, hops)),
            DMA((HALVES, heads, hops)),
            DMA((heads, hops)),
            DMA((heads, hops)),
            DMA((HALVES - 1, hops)),
            DMA((HALVES - 1, hops)),
            DMA((3, heads, hops)),
            DMA((3, heads, hops)),
            DMA((EARLY + 1, hops)),
            DMA((EARLY + 1, hops)),
            DMA((dp_count + hops,)),
            DMA((dp_count + hops,)),
            DMA((dp_count + hops,)),
            DMA((dp_count + hops,)),
            DMA((3,)),
            DMA((1,)),
        ],
        compiler_params=pltpu.CompilerParams(
            collective_id=0, has_side_effects=True, vmem_limit_bytes=44 << 20
        ),
    )(modulation, gains, condition, residual, query, key, value, residual_grad, mod_grad)


def results_kernel(factor, *refs):
    sources, sums_ref, targets, params_ref, sem = refs[:4], refs[4], refs[5:9], refs[9], refs[10]
    copies = [
        pltpu.make_async_copy(source, target, sem.at[i])
        for i, (source, target) in enumerate(zip(sources, targets))
    ]
    for copy in copies:
        copy.start()
    rows, own = params_ref.shape
    params_ref[...] = sums_ref[0:rows, 0:own] * factor
    for copy in copies:
        copy.wait()


def results(factor, own, parts):
    hbm = pl.BlockSpec(memory_space=pltpu.HBM)
    vmem = pl.BlockSpec(memory_space=VMEM)
    big = [jax.ShapeDtypeStruct(part.shape, part.dtype) for part in parts[:4]]
    return pl.pallas_call(
        functools.partial(results_kernel, factor),
        out_shape=(*big, jax.ShapeDtypeStruct((5, own), F32)),
        in_specs=[vmem] * 4 + [vmem],
        out_specs=(*([hbm] * 4), vmem),
        scratch_shapes=[DMA((4,))],
        compiler_params=pltpu.CompilerParams(vmem_limit_bytes=8 << 20),
    )(*parts)


def per_device(
    layout,
    residual,
    query_raw,
    key_raw,
    values,
    residual_grad,
    modulated_grad,
    condition,
    modulation,
    norm_gains,
):
    residual, query_raw, key_raw, values, residual_grad, modulated_grad = (
        pltpu.with_memory_space_constraint(x, pltpu.HBM)
        for x in (residual, query_raw, key_raw, values, residual_grad, modulated_grad)
    )
    condition, modulation, norm_gains = (
        pltpu.with_memory_space_constraint(x, pltpu.HBM)
        for x in (condition[0], modulation, norm_gains)
    )
    factor = (residual.shape[0] * lax.axis_size("seq") * lax.axis_size("dp")) ** (-0.5)
    return results(
        factor,
        modulation.shape[1],
        whole_block(
            layout,
            modulation,
            norm_gains,
            condition,
            residual,
            query_raw,
            key_raw,
            values,
            residual_grad,
            modulated_grad,
        ),
    )


def solution(mesh):
    layout = (8, 4, mesh.shape["dp"] // 32) if mesh.shape["dp"] >= 32 else (mesh.shape["dp"], 1, 1)
    rows = P(("seq", "dp"), None)
    columns = P(None, ("seq", "dp"))
    return jax.shard_map(
        functools.partial(per_device, layout),
        mesh=mesh,
        in_specs=(rows,) * 6 + (P("dp", None, None), columns, columns),
        out_specs=(rows,) * 4 + (columns,),
        check_vma=False,
    )
```

```python
import functools

import jax
import jax.numpy as jnp
from jax import lax
from jax.experimental import pallas as pl
from jax.experimental.pallas import tpu as pltpu
from jax.sharding import PartitionSpec as P

HEAD_DIM = 128
N_SEQ = 4
EPSILON = 1e-06
SCORE_SCALE = HEAD_DIM ** (-0.5)
MESH = pl.DeviceIdType.MESH
VMEM = pltpu.VMEM
DMA = pltpu.SemaphoreType.DMA
F32 = jnp.float32
BF16 = jnp.bfloat16
BLOCK = 256
CHUNK = 16
HALVES = 2
EARLY = 2
SPLIT = 2


def dot_nt(a, b):
    return lax.dot_general(a, b, (((1,), (1,)), ((), ())), preferred_element_type=F32)


def dot_nn(a, b):
    return lax.dot_general(a, b, (((1,), (0,)), ((), ())), preferred_element_type=F32)


def times(start, width):
    return pl.ds(pl.multiple_of(start, width), width)


def kernel(
    layout,
    modulation_hbm,
    gains_hbm,
    condition_hbm,
    residual_hbm,
    query_hbm,
    key_hbm,
    value_hbm,
    residual_grad_hbm,
    modulated_grad_hbm,
    input_grad_hbm,
    query_grad_hbm,
    key_grad_hbm,
    value_grad_hbm,
    sums_ref,
    residual_t,
    query_t,
    key_t,
    residual_grad_t,
    modulated_grad_t,
    attended_t,
    attended_grad_t,
    input_grad_t,
    query_out_t,
    key_out_t,
    scale_t,
    scale_out,
    query_back,
    key_back,
    query_own,
    key_own,
    modulated,
    query_h,
    key_h,
    value_h,
    scale_in,
    scale_h,
    query_n,
    key_n,
    weights_h,
    attended_h,
    grad_h,
    query_grad_h,
    key_grad_h,
    value_grad_h,
    query_total,
    key_total,
    value_total,
    gain_sums,
    modulation_ref,
    gains_ref,
    condition_ref,
    gather_z,
    gather_y,
    gather_x,
    got_z,
    got_y,
    got_x,
    mine,
    full,
    reduce_x,
    reduce_y,
    reduce_z,
    back_x,
    back_y,
    back_z,
    total_x,
    total_y,
    columns,
    column_rows,
    seq_parts,
    in_sem,
    own_sem,
    raw_send,
    raw_recv,
    scale_send,
    scale_recv,
    att_send,
    att_recv,
    grad_send,
    grad_recv,
    wide_send,
    wide_recv,
    back_send,
    back_recv,
    value_send,
    value_recv,
    gather_send,
    gather_recv,
    reduce_send,
    reduce_recv,
    out_sem,
    value_sem,
):
    n_z, n_y, n_x = layout
    stages = (("z", n_z - 1), ("y", n_y - 1), ("x", n_x - 1))
    dp_count = sum(count for _, count in stages)
    own = modulation_ref.shape[1]
    rows, width = residual_t.shape
    heads = key_h.shape[0]
    local = heads * HEAD_DIM
    tokens = key_h.shape[1]
    s = lax.axis_index("seq")
    d = lax.axis_index("dp")
    hops = range(1, N_SEQ)
    part_size = rows // HALVES
    part_queries = tokens // HALVES
    at_z, at_y, at_x = d % n_z, (d // n_z) % n_y, d // (n_z * n_y)
    block_y, block_x = own * n_z, own * n_z * n_y

    def peer(k):
        return (s + k) % N_SEQ

    def sender(k):
        return (s + N_SEQ - k) % N_SEQ

    def dp_partner(stage, k):
        if stage == "z":
            return (d // n_z) * n_z + (d % n_z + k) % n_z
        if stage == "y":
            row = (d // n_z) % n_y
            return d + ((row + k) % n_y - row) * n_z
        return (d + n_z * n_y * k) % (n_z * n_y * n_x)

    def send(src, dst, send_sem, recv_sem, device):
        return pltpu.make_async_remote_copy(
            src_ref=src,
            dst_ref=dst,
            send_sem=send_sem,
            recv_sem=recv_sem,
            device_id=device,
            device_id_type=MESH,
        )

    def head_columns(owner, h):
        return times((owner * heads + h) * HEAD_DIM, HEAD_DIM)

    def token_rows(owner):
        return times(owner * rows, rows)

    def part_rows(part):
        return pl.ds(part * part_size, part_size)

    def query_rows(part, owner):
        start = part * part_queries + owner * part_size
        return pl.ds(pl.multiple_of(start, part_size), part_size)

    def raw_refs(t, h, owner):
        at = head_columns(owner, h)
        if t in (0, 2):
            source, target = ((key_hbm, key_h), (value_hbm, value_h))[t // 2]
            return source.at[:, at], target.at[h, token_rows(s), :]
        if t == 1:
            target = query_h.at[query_rows(0, s), times(h * HEAD_DIM, HEAD_DIM)]
            return query_hbm.at[part_rows(0), at], target
        return (
            query_hbm.at[part_rows(1), times(owner * local, HEAD_DIM * heads)],
            query_h.at[query_rows(1, s), :],
        )

    def raw_copy(t, h, k):
        return send(
            *raw_refs(t, h, peer(k)),
            raw_send.at[t],
            raw_recv.at[t, h],
            {"seq": peer(k)},
        )

    def own_copy(t, h):
        return pltpu.make_async_copy(*raw_refs(t, h, s), own_sem.at[0])

    def all_of(ref, sem):
        pltpu.make_async_copy(ref, ref, sem).wait()

    three_rows, three_parts, three_local = 3 * rows, 3 * part_size, 3 * local

    def all_raw(t, h):
        at = times(h * HEAD_DIM, HEAD_DIM)
        if t == 1:
            ref = query_h.at[0:three_parts, at]
        elif t == 3:
            ref = query_h.at[0:three_parts, :]
        else:
            ref = (key_h, value_h)[t // 2].at[h, 0:three_rows, :]
        all_of(ref, raw_recv.at[t, h])

    def scale_copy(k):
        return send(
            scale_out,
            scale_in.at[s],
            scale_send.at[k - 1],
            scale_recv.at[k - 1],
            {"seq": peer(k)},
        )

    def att_copy(part, h, k):
        return send(
            attended_h.at[h, query_rows(part, peer(k)), :],
            attended_t.at[part_rows(part), head_columns(s, h)],
            att_send.at[part],
            att_recv.at[part],
            {"seq": peer(k)},
        )

    def grad_copy(part, k):
        return send(
            attended_grad_t.at[part_rows(part), times(peer(k) * local, HEAD_DIM * heads)],
            grad_h.at[query_rows(part, s), :],
            wide_send.at[part],
            wide_recv.at[part],
            {"seq": peer(k)},
        )

    def last_grad_copy(h, k):
        part = HALVES - 1
        return send(
            attended_grad_t.at[part_rows(part), head_columns(peer(k), h)],
            grad_h.at[query_rows(part, s), times(h * HEAD_DIM, HEAD_DIM)],
            grad_send.at[0],
            grad_recv.at[h],
            {"seq": peer(k)},
        )

    def back_copy(t, h, k, count=1):
        at = pl.ds(pl.multiple_of(h * HEAD_DIM, HEAD_DIM), count * HEAD_DIM)
        if t == 1:
            source = key_grad_h.at[token_rows(peer(k)), at]
            target = key_back.at[k - 1, :, at]
        else:
            source = query_grad_h.at[query_rows(t // 2, peer(k)), at]
            target = query_back.at[k - 1, part_rows(t // 2), at]
        return send(
            source,
            target,
            back_send.at[t],
            back_recv.at[t],
            {"seq": peer(k)},
        )

    def value_back(h, k, count=1):
        return send(
            value_grad_h.at[token_rows(peer(k)), pl.ds(pl.multiple_of(h * HEAD_DIM, HEAD_DIM), count * HEAD_DIM)],
            value_grad_hbm.at[
                :,
                pl.ds(pl.multiple_of((s * heads + h) * HEAD_DIM, HEAD_DIM), count * HEAD_DIM),
            ],
            value_send.at[0],
            value_recv.at[0],
            {"seq": peer(k)},
        )

    value_own = pltpu.make_async_copy(
        value_grad_h.at[token_rows(s), :],
        value_grad_hbm.at[:, times(s * local, HEAD_DIM * heads)],
        value_sem.at[0],
    )

    def start_raw(h):
        for t in range(3):
            for k in hops:
                raw_copy(t, h, k).start()

    def exchange(stage, sources, targets, send_sem, recv_sem, base):
        copies = [
            send(
                source,
                targets.at[k],
                send_sem.at[base + k],
                recv_sem.at[base + k],
                {"dp": dp_partner(stage, k + 1)},
            )
            for k, source in enumerate(sources)
        ]
        for copy in copies:
            copy.start()
        return copies

    def arrived(start, copies, targets):
        total = start
        for k, copy in enumerate(copies):
            copy.wait_recv()
            total = total + targets[k]
        return total

    def widened(ref, values, shift):
        ref[...] = jnp.zeros_like(ref)
        ref[:, 0 : values.shape[1]] = values
        ref[...] = pltpu.roll(ref[...], shift, 1)

    def window(values, first, count):
        lanes = values.shape[1]
        return pltpu.roll(values, (lanes - first) % lanes, 1)[:, 0:count]

    def start_back(t, h):
        for k in hops:
            back_copy(t, h, k).start()

    inputs = (
        (key_hbm, key_t),
        (query_hbm, query_t),
        (residual_hbm, residual_t),
        (residual_grad_hbm, residual_grad_t),
        (modulated_grad_hbm, modulated_grad_t),
    )
    loads = [
        pltpu.make_async_copy(src, dst, in_sem.at[i]) for i, (src, dst) in enumerate(inputs)
    ]
    small = (
        (modulation_hbm, modulation_ref),
        (gains_hbm, gains_ref),
        (condition_hbm, condition_ref),
    )
    small_loads = [
        pltpu.make_async_copy(src, dst, in_sem.at[len(inputs) + i])
        for i, (src, dst) in enumerate(small)
    ]
    partners = [{"seq": peer(k)} for k in hops]
    for stage, count in stages:
        partners += [{"dp": dp_partner(stage, k)} for k in range(1, count + 1)]
    barrier = pltpu.get_barrier_semaphore()
    for partner in partners:
        pl.semaphore_signal(barrier, inc=1, device_id=partner, device_id_type=MESH)
    for load in small_loads:
        load.start()
    for load in small_loads:
        load.wait()

    gather_z[...] = jnp.zeros_like(gather_z)
    gather_z[0:2, 0:own] = modulation_ref[...]
    gather_z[2:4, 0:own] = gains_ref[...]
    gather_z[...] = pltpu.roll(gather_z[...], at_z * own, 1)

    pl.semaphore_wait(barrier, len(partners))

    def scales():
        scale_t[:, rows:, :] = jnp.zeros((2, BLOCK - rows, HEAD_DIM), F32)
        scale_out[...] = jnp.zeros_like(scale_out)
        for t, source in ((0, key_t), (1, query_t)):
            loads[t].wait()

            @pl.loop(0, rows // CHUNK)
            def _(i):
                at = times(i * CHUNK, CHUNK)
                floats = source[at, :].astype(F32)
                mean = jnp.sum(floats * floats, axis=1, keepdims=True) * (1.0 / width)
                scale_t[t, at, :] = jnp.broadcast_to(
                    lax.rsqrt(mean + EPSILON), (CHUNK, HEAD_DIM)
                )

            scale_out[t : t + 1, :] = scale_t[t].T[0:1, :]
        for k in hops:
            scale_copy(k).start()
        scale_in[s] = scale_out[...]

    copies_z = exchange(
        "z", [gather_z] * (n_z - 1), got_z, gather_send, gather_recv, 0
    )
    start_raw(0)
    for load in loads:
        load.start()
    for t in range(3):
        for h in range(heads):
            own_copy(t, h).start()
    own_copy(3, 0).start()
    scales()
    widened(gather_y, arrived(gather_z[...], copies_z, got_z), at_y * block_y)
    copies_y = exchange(
        "y", [gather_y] * (n_y - 1), got_y, gather_send, gather_recv, n_z - 1
    )
    start_raw(1)
    widened(gather_x, arrived(gather_y[...], copies_y, got_y), at_x * block_x)
    copies_x = exchange(
        "x", [gather_x] * (n_x - 1), got_x, gather_send, gather_recv, n_z + n_y - 2
    )
    start_raw(2)
    mine[...] = arrived(gather_x[...], copies_x, got_x)
    gather_copies = copies_z + copies_y + copies_x
    full[s] = mine[0:4, :]
    full_copies = [
        send(
            mine.at[0:4, :],
            full.at[s],
            gather_send.at[dp_count + k - 1],
            gather_recv.at[dp_count + k - 1],
            {"seq": peer(k)},
        )
        for k in hops
    ]
    for copy in full_copies:
        copy.start()
    for h in range(3, heads):
        start_raw(h)
    for k in hops:
        raw_copy(3, 0, k).start()

    for k in hops:
        scale_copy(k).wait_recv()
    for owner in range(N_SEQ):
        for t in range(2):
            spread = jnp.broadcast_to(scale_in[owner, t : t + 1, :], (HEAD_DIM, BLOCK)).T
            if t == 0:
                scale_h[t, owner * rows : (owner + 1) * rows, :] = spread[0:rows, :]
            else:
                for part in range(HALVES):
                    at = part * part_queries + owner * part_size
                    scale_h[t, at : at + part_size, :] = spread[
                        part * part_size : (part + 1) * part_size, :
                    ]

    for part, sent in ((0, (0, 1, 2)), (1, ())):
        at = slice(part * part_queries, (part + 1) * part_queries)
        if part == 0:
            all_of(attended_t.at[:, 0:three_local], own_sem.at[0])
        else:
            all_raw(3, 0)

        @pl.loop(0, heads)
        def _(h):
            gain_at = times(h * HEAD_DIM, HEAD_DIM)
            for t in sent:
                all_raw(t, h)
            query_n[h, at, :] = (
                query_h[at, gain_at].astype(F32) * scale_h[1, at, :] * mine[2:3, gain_at]
            ).astype(BF16)
            if part == 0:
                key_n[h] = (key_h[h].astype(F32) * scale_h[0] * mine[3:4, gain_at]).astype(BF16)
            scores = dot_nt(key_n[h], query_n[h, at, :]) * SCORE_SCALE
            top = jnp.max(scores, axis=0, keepdims=True)
            raised = jnp.exp(scores - top)
            total = jnp.sum(raised, axis=0, keepdims=True)
            weights = raised * (1.0 / total)
            weights_h[h, :, at] = weights
            attended_h[h, at, :] = dot_nn(value_h[h].T, weights.astype(BF16)).T.astype(BF16)
            for k in hops:
                att_copy(part, h, k).start()
            attended_t[part_rows(part), head_columns(s, h)] = attended_h[
                h, query_rows(part, s), :
            ]

    for copy in full_copies:
        copy.wait_recv()
    for part in range(N_SEQ):
        at = slice(part * local, (part + 1) * local)
        modulated[:, at] = full[part, 0:2, :] + condition_ref[:, at]
    for load in loads[2:]:
        load.wait()
    columns[...] = jnp.zeros_like(columns)

    for part in range(HALVES):
        all_of(attended_t.at[part_rows(part), 0:three_local], att_recv.at[part])

        @pl.loop(part * part_size // CHUNK, (part + 1) * part_size // CHUNK)
        def _(i):
            at = times(i * CHUNK, CHUNK)
            gate_row = modulated[0:1, :]
            attended = attended_t[at, :].astype(F32)
            summed = residual_t[at, :].astype(F32) + gate_row * attended
            centered = summed - jnp.sum(summed, axis=1, keepdims=True) * (1.0 / width)
            norm_scale = lax.rsqrt(
                jnp.sum(centered * centered, axis=1, keepdims=True) * (1.0 / width) + EPSILON
            )
            normed = centered * norm_scale
            upstream = modulated_grad_t[at, :].astype(F32)
            scaled = upstream * (1.0 + modulated[1:2, :])
            stream_grad = residual_grad_t[at, :].astype(F32) + norm_scale * (
                scaled
                - jnp.sum(scaled, axis=1, keepdims=True) * (1.0 / width)
                - normed * (jnp.sum(scaled * normed, axis=1, keepdims=True) * (1.0 / width))
            )
            input_grad_t[at, :] = stream_grad.astype(BF16)
            attended_grad_t[at, :] = (stream_grad * gate_row).astype(BF16)
            for row, term in enumerate((stream_grad * attended, upstream, upstream * normed)):
                columns[row] += term[0:8, :] + term[8:16, :]

        if part < HALVES - 1:
            for k in hops:
                grad_copy(part, k).start()
        else:

            @pl.loop(0, heads)
            def _(h):
                for k in hops:
                    last_grad_copy(h, k).start()

        grad_h[query_rows(part, s), :] = attended_grad_t[
            part_rows(part), times(s * local, HEAD_DIM * heads)
        ]

    input_grad_out = pltpu.make_async_copy(input_grad_t, input_grad_hbm, out_sem.at[0])
    input_grad_out.start()
    column_rows[3:8, :] = jnp.zeros((5, width), F32)
    for row in range(3):
        column_rows[row : row + 1, :] = jnp.sum(columns[row], axis=0, keepdims=True)
    seq_copies = [
        send(
            column_rows.at[0:4, times(peer(k) * local, HEAD_DIM * heads)],
            seq_parts.at[k - 1],
            reduce_send.at[dp_count + k - 1],
            reduce_recv.at[dp_count + k - 1],
            {"seq": peer(k)},
        )
        for k in hops
    ]
    for copy in seq_copies:
        copy.start()
    gain_sums[0:3, :] = column_rows[0:3, times(s * local, HEAD_DIM * heads)]
    gain_sums[5:8, :] = jnp.zeros((3, local), F32)

    for part in range(HALVES - 1):
        all_of(grad_h.at[0:three_parts, :], wide_recv.at[part])

    @pl.loop(0, heads)
    def _(h):
        all_of(grad_h.at[0:three_parts, times(h * HEAD_DIM, HEAD_DIM)], grad_recv.at[h])
        at_head = times(h * HEAD_DIM, HEAD_DIM)
        keys_t = key_n[h].T
        key_total[...] = jnp.zeros_like(key_total)
        value_total[...] = jnp.zeros_like(value_total)
        gain_sums[3:4, at_head] = jnp.zeros((1, HEAD_DIM), F32)

        @pl.loop(0, tokens // BLOCK)
        def _(i):
            at = times(i * BLOCK, BLOCK)
            queries = query_n[h, at, :]
            grads = grad_h[at, at_head]
            weights = weights_h[h, :, at]
            product = grads.astype(F32) * attended_h[h, at, :].astype(F32)
            row_dot = jnp.sum(product.T, axis=0, keepdims=True)
            weight_grad = dot_nt(value_h[h], grads)
            score_grad = (weights * (weight_grad - row_dot) * SCORE_SCALE).astype(BF16)
            value_total[...] += dot_nn(weights.astype(BF16), grads)
            key_total[...] += dot_nn(score_grad, queries)
            query_grad = dot_nn(keys_t, score_grad).T
            query_total[at, :] = query_grad
            query_grad_h[at, at_head] = query_grad.astype(BF16)
            gain_sums[3:4, at_head] += jnp.sum(
                query_grad * (query_h[at, at_head].astype(F32) * scale_h[1, at, :]),
                axis=0,
                keepdims=True,
            )

        key_grad_h[:, at_head] = key_total[...].astype(BF16)
        value_grad_h[:, at_head] = value_total[...].astype(BF16)
        gain_sums[4:5, at_head] = jnp.sum(
            key_total[...] * (key_h[h].astype(F32) * scale_h[0]), axis=0, keepdims=True
        )

        @pl.when(h < EARLY)
        def _():
            for t in range(3):
                start_back(t, h)
            for k in hops:
                value_back(h, k).start()

        for part in range(HALVES):
            query_own[part_rows(part), at_head] = query_total[query_rows(part, s), :]
        key_own[:, at_head] = key_total[token_rows(s), :]

    value_own.start()

    def start_late(pieces):
        for t in pieces:
            for k in hops:
                back_copy(t, EARLY, k, heads - EARLY).start()

    for k, copy in enumerate(seq_copies):
        copy.wait_recv()
        gain_sums[0:3, :] += seq_parts[k, 0:3, :]
    sums = gain_sums[...]
    for k in range(1, n_x):
        reduce_x[k - 1] = window(sums, (at_x + k) % n_x * block_x, reduce_x.shape[2])
    copies_x = exchange(
        "x", [reduce_x.at[k] for k in range(n_x - 1)], back_x, reduce_send, reduce_recv, 0
    )
    start_late((0, 2))
    total_x[...] = arrived(window(sums, at_x * block_x, total_x.shape[1]), copies_x, back_x)
    sums = total_x[...]
    for k in range(1, n_y):
        reduce_y[k - 1] = window(sums, (at_y + k) % n_y * block_y, reduce_y.shape[2])
    copies_y = exchange(
        "y", [reduce_y.at[k] for k in range(n_y - 1)], back_y, reduce_send, reduce_recv, n_x - 1
    )
    start_late((1,))
    total_y[...] = arrived(window(sums, at_y * block_y, total_y.shape[1]), copies_y, back_y)
    sums = total_y[...]
    for k in range(1, n_z):
        reduce_z[k - 1] = window(sums, (at_z + k) % n_z * own, reduce_z.shape[2])
    copies_z = exchange(
        "z",
        [reduce_z.at[k] for k in range(n_z - 1)],
        back_z,
        reduce_send,
        reduce_recv,
        n_x + n_y - 2,
    )
    for k in hops:
        value_back(EARLY, k, heads - EARLY).start()
    sums_ref[...] = arrived(window(sums, at_z * own, sums_ref.shape[1]), copies_z, back_z)
    reduce_copies = copies_x + copies_y + copies_z

    for t in range(4):
        ref = attended_t.at[part_rows(0), 0:three_local] if t % 2 else attended_t.at[:, 0:three_local]
        all_of(ref, raw_send.at[t])
    for part in range(HALVES):
        all_of(attended_t.at[part_rows(0), 0:three_local], att_send.at[part])
    for sem in [wide_send.at[part] for part in range(HALVES - 1)] + [grad_send.at[0]]:
        all_of(attended_grad_t.at[part_rows(0), 0:three_local], sem)
    for k in hops:
        scale_copy(k).wait_send()
    for copy in gather_copies + full_copies + seq_copies:
        copy.wait_send()

    outs = []
    for t, (raw, back, own, out, out_hbm, scale_row, gain_row) in enumerate(
        (
            (query_t, query_back, query_own, query_out_t, query_grad_hbm, 1, 2),
            (key_t, key_back, key_own, key_out_t, key_grad_hbm, 0, 3),
        )
    ):

        for piece in ((0, 2), (1,))[t]:
            ref = key_back if piece == 1 else query_back.at[:, part_rows(piece // 2), :]
            all_of(ref, back_recv.at[piece])

        @pl.loop(0, rows // CHUNK)
        def _(i):
            at = times(i * CHUNK, CHUNK)
            inverse = scale_t[scale_row, at, 0:1]
            parts = []
            mean = jnp.zeros((CHUNK, 1), F32)
            for k in range(N_SEQ):
                block = sender(k)
                where = times(block * local, HEAD_DIM * heads)
                upstream = own[at, :] if k == 0 else back[k - 1, at, :].astype(F32)
                weighted = full[block, gain_row : gain_row + 1, :] * upstream
                floats = raw[at, where].astype(F32)
                mean = mean + jnp.sum(floats * weighted, axis=1, keepdims=True)
                parts.append((where, weighted, floats))
            factor = inverse * inverse * inverse * (mean * (1.0 / width))
            for where, weighted, floats in parts:
                out[at, where] = (inverse * weighted - floats * factor).astype(BF16)

        outs.append(pltpu.make_async_copy(out, out_hbm, out_sem.at[1 + t]))
        outs[-1].start()

    for t in range(3):
        count = three_rows if t == 1 else three_parts
        all_of(key_grad_h.at[0:count, :], back_send.at[t])
    for copy in reduce_copies:
        copy.wait_send()
    value_own.wait()
    all_of(value_grad_h.at[0:three_rows, :], value_send.at[0])
    all_of(value_grad_hbm.at[:, 0:three_local], value_recv.at[0])
    input_grad_out.wait()
    for out in outs:
        out.wait()


def whole_block(layout, modulation, gains, condition, residual, query, key, value, residual_grad, mod_grad):
    rows, width = residual.shape
    local = width // N_SEQ
    heads = local // HEAD_DIM
    tokens = rows * N_SEQ
    n_z, n_y, n_x = layout
    dp_count = n_z + n_y + n_x - 3
    token = VMEM((rows, width), BF16)
    by_head = VMEM((heads, tokens, HEAD_DIM), BF16)
    wide = VMEM((tokens, local), BF16)

    own = modulation.shape[1]
    wide_own, wide_z, wide_y = (
        -(-lanes // HEAD_DIM) * HEAD_DIM for lanes in (own, own * n_z, own * n_z * n_y)
    )
    hbm = pl.BlockSpec(memory_space=pl.ANY)
    vmem = pl.BlockSpec(memory_space=VMEM)
    big = jax.ShapeDtypeStruct((rows, width), BF16)
    hops = N_SEQ - 1
    return pl.pallas_call(
        functools.partial(kernel, layout),
        out_shape=(big, big, big, big, jax.ShapeDtypeStruct((8, wide_own), F32)),
        in_specs=[pl.BlockSpec(memory_space=pltpu.HBM)] * 9,
        out_specs=(hbm, hbm, hbm, hbm, vmem),
        scratch_shapes=[
            token,
            token,
            token,
            token,
            token,
            token,
            token,
            token,
            token,
            token,
            VMEM((2, BLOCK, HEAD_DIM), F32),
            VMEM((8, BLOCK), F32),
            VMEM((hops, rows, local), BF16),
            VMEM((hops, rows, local), BF16),
            VMEM((rows, local), F32),
            VMEM((rows, local), F32),
            VMEM((2, width), F32),
            wide,
            by_head,
            by_head,
            VMEM((N_SEQ, 8, BLOCK), F32),
            VMEM((2, tokens, HEAD_DIM), F32),
            by_head,
            by_head,
            VMEM((heads, tokens, tokens), F32),
            by_head,
            wide,
            wide,
            wide,
            wide,
            VMEM((tokens, HEAD_DIM), F32),
            VMEM((tokens, HEAD_DIM), F32),
            VMEM((tokens, HEAD_DIM), F32),
            VMEM((8, local), F32),
            VMEM(modulation.shape, F32),
            VMEM(gains.shape, F32),
            VMEM(condition.shape, F32),
            VMEM((8, wide_z), F32),
            VMEM((8, wide_y), F32),
            VMEM((8, local), F32),
            VMEM((max(n_z - 1, 1), 8, wide_z), F32),
            VMEM((max(n_y - 1, 1), 8, wide_y), F32),
            VMEM((max(n_x - 1, 1), 8, local), F32),
            VMEM((8, local), F32),
            VMEM((N_SEQ, 4, local), F32),
            VMEM((max(n_x - 1, 1), 8, wide_y), F32),
            VMEM((max(n_y - 1, 1), 8, wide_z), F32),
            VMEM((max(n_z - 1, 1), 8, wide_own), F32),
            VMEM((max(n_x - 1, 1), 8, wide_y), F32),
            VMEM((max(n_y - 1, 1), 8, wide_z), F32),
            VMEM((max(n_z - 1, 1), 8, wide_own), F32),
            VMEM((8, wide_y), F32),
            VMEM((8, wide_z), F32),
            VMEM((3, 8, width), F32),
            VMEM((8, width), F32),
            VMEM((hops, 4, local), F32),
            DMA((8,)),
            DMA((1,)),
            DMA((4,)),
            DMA((4, heads)),
            DMA((hops,)),
            DMA((hops,)),
            DMA((HALVES,)),
            DMA((HALVES,)),
            DMA((1,)),
            DMA((heads,)),
            DMA((HALVES - 1,)),
            DMA((HALVES - 1,)),
            DMA((3,)),
            DMA((3,)),
            DMA((1,)),
            DMA((1,)),
            DMA((dp_count + hops,)),
            DMA((dp_count + hops,)),
            DMA((dp_count + hops,)),
            DMA((dp_count + hops,)),
            DMA((3,)),
            DMA((1,)),
        ],
        compiler_params=pltpu.CompilerParams(
            collective_id=0, has_side_effects=True, vmem_limit_bytes=44 << 20
        ),
    )(modulation, gains, condition, residual, query, key, value, residual_grad, mod_grad)


def results_kernel(factor, *refs):
    sources, sums_ref, targets, params_ref, sem = refs[:4], refs[4], refs[5:9], refs[9], refs[10]
    copies = [
        pltpu.make_async_copy(source, target, sem.at[i])
        for i, (source, target) in enumerate(zip(sources, targets))
    ]
    for copy in copies:
        copy.start()
    rows, own = params_ref.shape
    params_ref[...] = sums_ref[0:rows, 0:own] * factor
    for copy in copies:
        copy.wait()


def results(factor, own, parts):
    hbm = pl.BlockSpec(memory_space=pltpu.HBM)
    vmem = pl.BlockSpec(memory_space=VMEM)
    big = [jax.ShapeDtypeStruct(part.shape, part.dtype) for part in parts[:4]]
    return pl.pallas_call(
        functools.partial(results_kernel, factor),
        out_shape=(*big, jax.ShapeDtypeStruct((5, own), F32)),
        in_specs=[vmem] * 4 + [vmem],
        out_specs=(*([hbm] * 4), vmem),
        scratch_shapes=[DMA((4,))],
        compiler_params=pltpu.CompilerParams(vmem_limit_bytes=8 << 20),
    )(*parts)


def per_device(
    layout,
    residual,
    query_raw,
    key_raw,
    values,
    residual_grad,
    modulated_grad,
    condition,
    modulation,
    norm_gains,
):
    residual, query_raw, key_raw, values, residual_grad, modulated_grad = (
        pltpu.with_memory_space_constraint(x, pltpu.HBM)
        for x in (residual, query_raw, key_raw, values, residual_grad, modulated_grad)
    )
    condition, modulation, norm_gains = (
        pltpu.with_memory_space_constraint(x, pltpu.HBM)
        for x in (condition[0], modulation, norm_gains)
    )
    factor = (residual.shape[0] * lax.axis_size("seq") * lax.axis_size("dp")) ** (-0.5)
    return results(
        factor,
        modulation.shape[1],
        whole_block(
            layout,
            modulation,
            norm_gains,
            condition,
            residual,
            query_raw,
            key_raw,
            values,
            residual_grad,
            modulated_grad,
        ),
    )


def solution(mesh):
    layout = (8, 4, mesh.shape["dp"] // 32) if mesh.shape["dp"] >= 32 else (mesh.shape["dp"], 1, 1)
    rows = P(("seq", "dp"), None)
    columns = P(None, ("seq", "dp"))
    return jax.shard_map(
        functools.partial(per_device, layout),
        mesh=mesh,
        in_specs=(rows,) * 6 + (P("dp", None, None), columns, columns),
        out_specs=(rows,) * 4 + (columns,),
        check_vma=False,
    )
```

```python
import functools

import jax
import jax.numpy as jnp
from jax import lax
from jax.experimental import pallas as pl
from jax.experimental.pallas import tpu as pltpu
from jax.sharding import PartitionSpec as P

HEAD_DIM = 128
N_SEQ = 4
EPSILON = 1e-06
SCORE_SCALE = HEAD_DIM ** (-0.5)
MESH = pl.DeviceIdType.MESH
VMEM = pltpu.VMEM
DMA = pltpu.SemaphoreType.DMA
F32 = jnp.float32
BF16 = jnp.bfloat16
BLOCK = 256
CHUNK = 16
HALVES = 2
EARLY = 2
SPLIT = 2


def dot_nt(a, b):
    return lax.dot_general(a, b, (((1,), (1,)), ((), ())), preferred_element_type=F32)


def dot_nn(a, b):
    return lax.dot_general(a, b, (((1,), (0,)), ((), ())), preferred_element_type=F32)


def times(start, width):
    return pl.ds(pl.multiple_of(start, width), width)


def kernel(
    layout,
    modulation_hbm,
    gains_hbm,
    condition_hbm,
    residual_hbm,
    query_hbm,
    key_hbm,
    value_hbm,
    residual_grad_hbm,
    modulated_grad_hbm,
    input_grad_hbm,
    query_grad_hbm,
    key_grad_hbm,
    value_grad_hbm,
    sums_ref,
    residual_t,
    query_t,
    key_t,
    residual_grad_t,
    modulated_grad_t,
    attended_t,
    attended_grad_t,
    input_grad_t,
    query_out_t,
    key_out_t,
    scale_t,
    scale_out,
    query_back,
    key_back,
    query_own,
    key_own,
    modulated,
    query_h,
    key_h,
    value_h,
    scale_in,
    scale_h,
    query_n,
    key_n,
    weights_h,
    attended_h,
    grad_h,
    query_grad_h,
    key_grad_h,
    value_grad_h,
    query_total,
    key_total,
    value_total,
    gain_sums,
    modulation_ref,
    gains_ref,
    condition_ref,
    gather_z,
    gather_y,
    gather_x,
    got_z,
    got_y,
    got_x,
    mine,
    full,
    reduce_x,
    reduce_y,
    reduce_z,
    back_x,
    back_y,
    back_z,
    total_x,
    total_y,
    columns,
    column_rows,
    seq_parts,
    in_sem,
    own_sem,
    raw_send,
    raw_recv,
    scale_send,
    scale_recv,
    att_send,
    att_recv,
    grad_send,
    grad_recv,
    wide_send,
    wide_recv,
    back_send,
    back_recv,
    value_send,
    value_recv,
    gather_send,
    gather_recv,
    reduce_send,
    reduce_recv,
    out_sem,
    value_sem,
):
    n_z, n_y, n_x = layout
    stages = (("z", n_z - 1), ("y", n_y - 1), ("x", n_x - 1))
    own = modulation_ref.shape[1]
    rows, width = residual_t.shape
    heads = key_h.shape[0]
    local = heads * HEAD_DIM
    tokens = key_h.shape[1]
    s = lax.axis_index("seq")
    d = lax.axis_index("dp")
    hops = range(1, N_SEQ)
    part_size = rows // HALVES
    part_queries = tokens // HALVES
    at_z, at_y, at_x = d % n_z, (d // n_z) % n_y, d // (n_z * n_y)
    block_y, block_x = own * n_z, own * n_z * n_y

    def peer(k):
        return (s + k) % N_SEQ

    def sender(k):
        return (s + N_SEQ - k) % N_SEQ

    def dp_partner(stage, k):
        if stage == "z":
            return (d // n_z) * n_z + (d % n_z + k) % n_z
        if stage == "y":
            row = (d // n_z) % n_y
            return d + ((row + k) % n_y - row) * n_z
        return (d + n_z * n_y * k) % (n_z * n_y * n_x)

    def send(src, dst, send_sem, recv_sem, device):
        return pltpu.make_async_remote_copy(
            src_ref=src,
            dst_ref=dst,
            send_sem=send_sem,
            recv_sem=recv_sem,
            device_id=device,
            device_id_type=MESH,
        )

    def head_columns(owner, h):
        return times((owner * heads + h) * HEAD_DIM, HEAD_DIM)

    def token_rows(owner):
        return times(owner * rows, rows)

    def part_rows(part):
        return pl.ds(part * part_size, part_size)

    def query_rows(part, owner):
        start = part * part_queries + owner * part_size
        return pl.ds(pl.multiple_of(start, part_size), part_size)

    def raw_refs(t, h, owner):
        at = head_columns(owner, h)
        if t in (0, 2):
            source, target = ((key_hbm, key_h), (value_hbm, value_h))[t // 2]
            return source.at[:, at], target.at[h, token_rows(s), :]
        if t == 1:
            target = query_h.at[query_rows(0, s), times(h * HEAD_DIM, HEAD_DIM)]
            return query_hbm.at[part_rows(0), at], target
        return (
            query_hbm.at[part_rows(1), times(owner * local, HEAD_DIM * heads)],
            query_h.at[query_rows(1, s), :],
        )

    def raw_copy(t, h, k):
        return send(
            *raw_refs(t, h, peer(k)),
            raw_send.at[t],
            raw_recv.at[t, h],
            {"seq": peer(k)},
        )

    def own_copy(t, h):
        return pltpu.make_async_copy(*raw_refs(t, h, s), own_sem.at[0])

    def all_of(ref, sem):
        pltpu.make_async_copy(ref, ref, sem).wait()

    three_rows, three_parts, three_local = 3 * rows, 3 * part_size, 3 * local

    def all_raw(t, h):
        at = times(h * HEAD_DIM, HEAD_DIM)
        if t == 1:
            ref = query_h.at[0:three_parts, at]
        elif t == 3:
            ref = query_h.at[0:three_parts, :]
        else:
            ref = (key_h, value_h)[t // 2].at[h, 0:three_rows, :]
        all_of(ref, raw_recv.at[t, h])

    def scale_copy(k):
        return send(
            scale_out,
            scale_in.at[s],
            scale_send.at[0],
            scale_recv.at[0],
            {"seq": peer(k)},
        )

    def att_copy(part, h, k):
        return send(
            attended_h.at[h, query_rows(part, peer(k)), :],
            attended_t.at[part_rows(part), head_columns(s, h)],
            att_send.at[part],
            att_recv.at[part],
            {"seq": peer(k)},
        )

    def grad_copy(part, k):
        return send(
            attended_grad_t.at[part_rows(part), times(peer(k) * local, HEAD_DIM * heads)],
            grad_h.at[query_rows(part, s), :],
            wide_send.at[part],
            wide_recv.at[part],
            {"seq": peer(k)},
        )

    def last_grad_copy(h, k):
        part = HALVES - 1
        return send(
            attended_grad_t.at[part_rows(part), head_columns(peer(k), h)],
            grad_h.at[query_rows(part, s), times(h * HEAD_DIM, HEAD_DIM)],
            grad_send.at[0],
            grad_recv.at[h],
            {"seq": peer(k)},
        )

    def back_copy(t, h, k, count=1):
        at = pl.ds(pl.multiple_of(h * HEAD_DIM, HEAD_DIM), count * HEAD_DIM)
        if t == 1:
            source = key_grad_h.at[token_rows(peer(k)), at]
            target = key_back.at[k - 1, :, at]
        else:
            source = query_grad_h.at[query_rows(t // 2, peer(k)), at]
            target = query_back.at[k - 1, part_rows(t // 2), at]
        return send(
            source,
            target,
            back_send.at[t],
            back_recv.at[t],
            {"seq": peer(k)},
        )

    def value_back(h, k, count=1):
        return send(
            value_grad_h.at[token_rows(peer(k)), pl.ds(pl.multiple_of(h * HEAD_DIM, HEAD_DIM), count * HEAD_DIM)],
            value_grad_hbm.at[
                :,
                pl.ds(pl.multiple_of((s * heads + h) * HEAD_DIM, HEAD_DIM), count * HEAD_DIM),
            ],
            value_send.at[0],
            value_recv.at[0],
            {"seq": peer(k)},
        )

    value_own = pltpu.make_async_copy(
        value_grad_h.at[token_rows(s), :],
        value_grad_hbm.at[:, times(s * local, HEAD_DIM * heads)],
        value_sem.at[0],
    )

    def start_raw(h):
        for t in range(3):
            for k in hops:
                raw_copy(t, h, k).start()

    def exchange(stage, sources, targets, send_sem, recv_sem):
        for k, source in enumerate(sources):
            send(
                source, targets.at[k], send_sem, recv_sem, {"dp": dp_partner(stage, k + 1)}
            ).start()
        return [(targets, send_sem, recv_sem)] if sources else []

    def arrived(start, group):
        total = start
        for targets, _, recv_sem in group:
            all_of(targets, recv_sem)
            for k in range(targets.shape[0]):
                total = total + targets[k]
        return total

    def sent(groups):
        for targets, send_sem, _ in groups:
            all_of(targets, send_sem)

    def widened(ref, values, shift):
        ref[...] = jnp.zeros_like(ref)
        ref[:, 0 : values.shape[1]] = values
        ref[...] = pltpu.roll(ref[...], shift, 1)

    def window(values, first, count):
        lanes = values.shape[1]
        return pltpu.roll(values, (lanes - first) % lanes, 1)[:, 0:count]

    def start_back(t, h):
        for k in hops:
            back_copy(t, h, k).start()

    inputs = (
        (key_hbm, key_t),
        (query_hbm, query_t),
        (residual_hbm, residual_t),
        (residual_grad_hbm, residual_grad_t),
        (modulated_grad_hbm, modulated_grad_t),
    )
    loads = [
        pltpu.make_async_copy(src, dst, in_sem.at[i]) for i, (src, dst) in enumerate(inputs)
    ]
    small = (
        (modulation_hbm, modulation_ref),
        (gains_hbm, gains_ref),
        (condition_hbm, condition_ref),
    )
    small_loads = [
        pltpu.make_async_copy(src, dst, in_sem.at[len(inputs) + i])
        for i, (src, dst) in enumerate(small)
    ]
    partners = [{"seq": peer(k)} for k in hops]
    for stage, count in stages:
        partners += [{"dp": dp_partner(stage, k)} for k in range(1, count + 1)]
    barrier = pltpu.get_barrier_semaphore()
    for partner in partners:
        pl.semaphore_signal(barrier, inc=1, device_id=partner, device_id_type=MESH)
    for load in small_loads:
        load.start()
    for load in small_loads:
        load.wait()

    gather_z[...] = jnp.zeros_like(gather_z)
    gather_z[0:2, 0:own] = modulation_ref[...]
    gather_z[2:4, 0:own] = gains_ref[...]
    gather_z[...] = pltpu.roll(gather_z[...], at_z * own, 1)

    pl.semaphore_wait(barrier, len(partners))

    def scales():
        scale_t[:, rows:, :] = jnp.zeros((2, BLOCK - rows, HEAD_DIM), F32)
        scale_out[...] = jnp.zeros_like(scale_out)
        for t, source in ((0, key_t), (1, query_t)):
            loads[t].wait()

            @pl.loop(0, rows // CHUNK)
            def _(i):
                at = times(i * CHUNK, CHUNK)
                floats = source[at, :].astype(F32)
                mean = jnp.sum(floats * floats, axis=1, keepdims=True) * (1.0 / width)
                scale_t[t, at, :] = jnp.broadcast_to(
                    lax.rsqrt(mean + EPSILON), (CHUNK, HEAD_DIM)
                )

            scale_out[t : t + 1, :] = scale_t[t].T[0:1, :]
        for k in hops:
            scale_copy(k).start()
        scale_in[s] = scale_out[...]

    copies_z = exchange(
        "z", [gather_z] * (n_z - 1), got_z, gather_send.at[0], gather_recv.at[0]
    )
    start_raw(0)
    for load in loads:
        load.start()
    for t in range(3):
        for h in range(heads):
            own_copy(t, h).start()
    own_copy(3, 0).start()
    scales()
    widened(gather_y, arrived(gather_z[...], copies_z), at_y * block_y)
    copies_y = exchange(
        "y", [gather_y] * (n_y - 1), got_y, gather_send.at[1], gather_recv.at[1]
    )
    start_raw(1)
    widened(gather_x, arrived(gather_y[...], copies_y), at_x * block_x)
    copies_x = exchange(
        "x", [gather_x] * (n_x - 1), got_x, gather_send.at[2], gather_recv.at[2]
    )
    start_raw(2)
    mine[...] = arrived(gather_x[...], copies_x)
    gather_copies = copies_z + copies_y + copies_x
    full[s] = mine[0:4, :]
    full_copies = [
        send(
            mine.at[0:4, :],
            full.at[s],
            gather_send.at[3],
            gather_recv.at[3],
            {"seq": peer(k)},
        )
        for k in hops
    ]
    for copy in full_copies:
        copy.start()
    for h in range(3, heads):
        start_raw(h)
    for k in hops:
        raw_copy(3, 0, k).start()

    all_of(scale_in.at[0:3], scale_recv.at[0])
    for owner in range(N_SEQ):
        for t in range(2):
            spread = jnp.broadcast_to(scale_in[owner, t : t + 1, :], (HEAD_DIM, BLOCK)).T
            if t == 0:
                scale_h[t, owner * rows : (owner + 1) * rows, :] = spread[0:rows, :]
            else:
                for part in range(HALVES):
                    at = part * part_queries + owner * part_size
                    scale_h[t, at : at + part_size, :] = spread[
                        part * part_size : (part + 1) * part_size, :
                    ]

    for part, pieces in ((0, (0, 1, 2)), (1, ())):
        at = slice(part * part_queries, (part + 1) * part_queries)
        if part == 0:
            all_of(attended_t.at[:, 0:three_local], own_sem.at[0])
        else:
            all_raw(3, 0)

        @pl.loop(0, heads)
        def _(h):
            gain_at = times(h * HEAD_DIM, HEAD_DIM)
            for t in pieces:
                all_raw(t, h)
            query_n[h, at, :] = (
                query_h[at, gain_at].astype(F32) * scale_h[1, at, :] * mine[2:3, gain_at]
            ).astype(BF16)
            if part == 0:
                key_n[h] = (key_h[h].astype(F32) * scale_h[0] * mine[3:4, gain_at]).astype(BF16)
            scores = dot_nt(key_n[h], query_n[h, at, :]) * SCORE_SCALE
            top = jnp.max(scores, axis=0, keepdims=True)
            raised = jnp.exp(scores - top)
            total = jnp.sum(raised, axis=0, keepdims=True)
            weights = raised * (1.0 / total)
            weights_h[h, :, at] = weights
            attended_h[h, at, :] = dot_nn(value_h[h].T, weights.astype(BF16)).T.astype(BF16)
            for k in hops:
                att_copy(part, h, k).start()
            attended_t[part_rows(part), head_columns(s, h)] = attended_h[
                h, query_rows(part, s), :
            ]

    all_of(full.at[0:3], gather_recv.at[3])
    for part in range(N_SEQ):
        at = slice(part * local, (part + 1) * local)
        modulated[:, at] = full[part, 0:2, :] + condition_ref[:, at]
    for load in loads[2:]:
        load.wait()
    columns[...] = jnp.zeros_like(columns)

    for part in range(HALVES):
        all_of(attended_t.at[part_rows(part), 0:three_local], att_recv.at[part])

        @pl.loop(part * part_size // CHUNK, (part + 1) * part_size // CHUNK)
        def _(i):
            at = times(i * CHUNK, CHUNK)
            gate_row = modulated[0:1, :]
            attended = attended_t[at, :].astype(F32)
            summed = residual_t[at, :].astype(F32) + gate_row * attended
            centered = summed - jnp.sum(summed, axis=1, keepdims=True) * (1.0 / width)
            norm_scale = lax.rsqrt(
                jnp.sum(centered * centered, axis=1, keepdims=True) * (1.0 / width) + EPSILON
            )
            normed = centered * norm_scale
            upstream = modulated_grad_t[at, :].astype(F32)
            scaled = upstream * (1.0 + modulated[1:2, :])
            stream_grad = residual_grad_t[at, :].astype(F32) + norm_scale * (
                scaled
                - jnp.sum(scaled, axis=1, keepdims=True) * (1.0 / width)
                - normed * (jnp.sum(scaled * normed, axis=1, keepdims=True) * (1.0 / width))
            )
            input_grad_t[at, :] = stream_grad.astype(BF16)
            attended_grad_t[at, :] = (stream_grad * gate_row).astype(BF16)
            for row, term in enumerate((stream_grad * attended, upstream, upstream * normed)):
                columns[row] += term[0:8, :] + term[8:16, :]

        if part < HALVES - 1:
            for k in hops:
                grad_copy(part, k).start()
        else:

            @pl.loop(0, heads)
            def _(h):
                for k in hops:
                    last_grad_copy(h, k).start()

        grad_h[query_rows(part, s), :] = attended_grad_t[
            part_rows(part), times(s * local, HEAD_DIM * heads)
        ]

    input_grad_out = pltpu.make_async_copy(input_grad_t, input_grad_hbm, out_sem.at[0])
    input_grad_out.start()
    column_rows[3:8, :] = jnp.zeros((5, width), F32)
    for row in range(3):
        column_rows[row : row + 1, :] = jnp.sum(columns[row], axis=0, keepdims=True)
    seq_copies = [
        send(
            column_rows.at[0:4, times(peer(k) * local, HEAD_DIM * heads)],
            seq_parts.at[k - 1],
            reduce_send.at[3],
            reduce_recv.at[3],
            {"seq": peer(k)},
        )
        for k in hops
    ]
    for copy in seq_copies:
        copy.start()
    gain_sums[0:3, :] = column_rows[0:3, times(s * local, HEAD_DIM * heads)]
    gain_sums[5:8, :] = jnp.zeros((3, local), F32)

    for part in range(HALVES - 1):
        all_of(grad_h.at[0:three_parts, :], wide_recv.at[part])

    @pl.loop(0, heads)
    def _(h):
        all_of(grad_h.at[0:three_parts, times(h * HEAD_DIM, HEAD_DIM)], grad_recv.at[h])
        at_head = times(h * HEAD_DIM, HEAD_DIM)
        keys_t = key_n[h].T
        key_total[...] = jnp.zeros_like(key_total)
        value_total[...] = jnp.zeros_like(value_total)
        gain_sums[3:4, at_head] = jnp.zeros((1, HEAD_DIM), F32)

        @pl.loop(0, tokens // BLOCK)
        def _(i):
            at = times(i * BLOCK, BLOCK)
            queries = query_n[h, at, :]
            grads = grad_h[at, at_head]
            weights = weights_h[h, :, at]
            product = grads.astype(F32) * attended_h[h, at, :].astype(F32)
            row_dot = jnp.sum(product.T, axis=0, keepdims=True)
            weight_grad = dot_nt(value_h[h], grads)
            score_grad = (weights * (weight_grad - row_dot) * SCORE_SCALE).astype(BF16)
            value_total[...] += dot_nn(weights.astype(BF16), grads)
            key_total[...] += dot_nn(score_grad, queries)
            query_grad = dot_nn(keys_t, score_grad).T
            query_total[at, :] = query_grad
            query_grad_h[at, at_head] = query_grad.astype(BF16)
            gain_sums[3:4, at_head] += jnp.sum(
                query_grad * (query_h[at, at_head].astype(F32) * scale_h[1, at, :]),
                axis=0,
                keepdims=True,
            )

        key_grad_h[:, at_head] = key_total[...].astype(BF16)
        value_grad_h[:, at_head] = value_total[...].astype(BF16)
        gain_sums[4:5, at_head] = jnp.sum(
            key_total[...] * (key_h[h].astype(F32) * scale_h[0]), axis=0, keepdims=True
        )

        @pl.when(h < EARLY)
        def _():
            for t in range(3):
                start_back(t, h)
            for k in hops:
                value_back(h, k).start()

        for part in range(HALVES):
            query_own[part_rows(part), at_head] = query_total[query_rows(part, s), :]
        key_own[:, at_head] = key_total[token_rows(s), :]

    value_own.start()

    def start_late(pieces):
        for t in pieces:
            for k in hops:
                back_copy(t, EARLY, k, heads - EARLY).start()

    all_of(seq_parts, reduce_recv.at[3])
    for k in range(N_SEQ - 1):
        gain_sums[0:3, :] += seq_parts[k, 0:3, :]
    sums = gain_sums[...]
    for k in range(1, n_x):
        reduce_x[k - 1] = window(sums, (at_x + k) % n_x * block_x, reduce_x.shape[2])
    copies_x = exchange(
        "x", [reduce_x.at[k] for k in range(n_x - 1)], back_x, reduce_send.at[0], reduce_recv.at[0]
    )
    start_late((0, 2))
    total_x[...] = arrived(window(sums, at_x * block_x, total_x.shape[1]), copies_x)
    sums = total_x[...]
    for k in range(1, n_y):
        reduce_y[k - 1] = window(sums, (at_y + k) % n_y * block_y, reduce_y.shape[2])
    copies_y = exchange(
        "y", [reduce_y.at[k] for k in range(n_y - 1)], back_y, reduce_send.at[1], reduce_recv.at[1]
    )
    start_late((1,))
    total_y[...] = arrived(window(sums, at_y * block_y, total_y.shape[1]), copies_y)
    sums = total_y[...]
    for k in range(1, n_z):
        reduce_z[k - 1] = window(sums, (at_z + k) % n_z * own, reduce_z.shape[2])
    copies_z = exchange(
        "z",
        [reduce_z.at[k] for k in range(n_z - 1)],
        back_z,
        reduce_send.at[2],
        reduce_recv.at[2],
    )
    for k in hops:
        value_back(EARLY, k, heads - EARLY).start()
    sums_ref[...] = arrived(window(sums, at_z * own, sums_ref.shape[1]), copies_z)
    reduce_copies = copies_x + copies_y + copies_z

    for t in range(4):
        ref = attended_t.at[part_rows(0), 0:three_local] if t % 2 else attended_t.at[:, 0:three_local]
        all_of(ref, raw_send.at[t])
    for part in range(HALVES):
        all_of(attended_t.at[part_rows(0), 0:three_local], att_send.at[part])
    for sem in [wide_send.at[part] for part in range(HALVES - 1)] + [grad_send.at[0]]:
        all_of(attended_grad_t.at[part_rows(0), 0:three_local], sem)
    all_of(scale_in.at[0:3], scale_send.at[0])
    sent(gather_copies)
    all_of(full.at[0:3], gather_send.at[3])
    all_of(seq_parts, reduce_send.at[3])

    outs = []
    for t, (raw, back, own, out, out_hbm, scale_row, gain_row) in enumerate(
        (
            (query_t, query_back, query_own, query_out_t, query_grad_hbm, 1, 2),
            (key_t, key_back, key_own, key_out_t, key_grad_hbm, 0, 3),
        )
    ):

        for piece in ((0, 2), (1,))[t]:
            ref = key_back if piece == 1 else query_back.at[:, part_rows(piece // 2), :]
            all_of(ref, back_recv.at[piece])

        @pl.loop(0, rows // CHUNK)
        def _(i):
            at = times(i * CHUNK, CHUNK)
            inverse = scale_t[scale_row, at, 0:1]
            parts = []
            mean = jnp.zeros((CHUNK, 1), F32)
            for k in range(N_SEQ):
                block = sender(k)
                where = times(block * local, HEAD_DIM * heads)
                upstream = own[at, :] if k == 0 else back[k - 1, at, :].astype(F32)
                weighted = full[block, gain_row : gain_row + 1, :] * upstream
                floats = raw[at, where].astype(F32)
                mean = mean + jnp.sum(floats * weighted, axis=1, keepdims=True)
                parts.append((where, weighted, floats))
            factor = inverse * inverse * inverse * (mean * (1.0 / width))
            for where, weighted, floats in parts:
                out[at, where] = (inverse * weighted - floats * factor).astype(BF16)

        outs.append(pltpu.make_async_copy(out, out_hbm, out_sem.at[1 + t]))
        outs[-1].start()

    for t in range(3):
        count = three_rows if t == 1 else three_parts
        all_of(key_grad_h.at[0:count, :], back_send.at[t])
    sent(reduce_copies)
    value_own.wait()
    all_of(value_grad_h.at[0:three_rows, :], value_send.at[0])
    all_of(value_grad_hbm.at[:, 0:three_local], value_recv.at[0])
    input_grad_out.wait()
    for out in outs:
        out.wait()


def whole_block(layout, modulation, gains, condition, residual, query, key, value, residual_grad, mod_grad):
    rows, width = residual.shape
    local = width // N_SEQ
    heads = local // HEAD_DIM
    tokens = rows * N_SEQ
    n_z, n_y, n_x = layout
    token = VMEM((rows, width), BF16)
    by_head = VMEM((heads, tokens, HEAD_DIM), BF16)
    wide = VMEM((tokens, local), BF16)

    own = modulation.shape[1]
    wide_own, wide_z, wide_y = (
        -(-lanes // HEAD_DIM) * HEAD_DIM for lanes in (own, own * n_z, own * n_z * n_y)
    )
    hbm = pl.BlockSpec(memory_space=pl.ANY)
    vmem = pl.BlockSpec(memory_space=VMEM)
    big = jax.ShapeDtypeStruct((rows, width), BF16)
    hops = N_SEQ - 1
    return pl.pallas_call(
        functools.partial(kernel, layout),
        out_shape=(big, big, big, big, jax.ShapeDtypeStruct((8, wide_own), F32)),
        in_specs=[pl.BlockSpec(memory_space=pltpu.HBM)] * 9,
        out_specs=(hbm, hbm, hbm, hbm, vmem),
        scratch_shapes=[
            token,
            token,
            token,
            token,
            token,
            token,
            token,
            token,
            token,
            token,
            VMEM((2, BLOCK, HEAD_DIM), F32),
            VMEM((8, BLOCK), F32),
            VMEM((hops, rows, local), BF16),
            VMEM((hops, rows, local), BF16),
            VMEM((rows, local), F32),
            VMEM((rows, local), F32),
            VMEM((2, width), F32),
            wide,
            by_head,
            by_head,
            VMEM((N_SEQ, 8, BLOCK), F32),
            VMEM((2, tokens, HEAD_DIM), F32),
            by_head,
            by_head,
            VMEM((heads, tokens, tokens), F32),
            by_head,
            wide,
            wide,
            wide,
            wide,
            VMEM((tokens, HEAD_DIM), F32),
            VMEM((tokens, HEAD_DIM), F32),
            VMEM((tokens, HEAD_DIM), F32),
            VMEM((8, local), F32),
            VMEM(modulation.shape, F32),
            VMEM(gains.shape, F32),
            VMEM(condition.shape, F32),
            VMEM((8, wide_z), F32),
            VMEM((8, wide_y), F32),
            VMEM((8, local), F32),
            VMEM((max(n_z - 1, 1), 8, wide_z), F32),
            VMEM((max(n_y - 1, 1), 8, wide_y), F32),
            VMEM((max(n_x - 1, 1), 8, local), F32),
            VMEM((8, local), F32),
            VMEM((N_SEQ, 4, local), F32),
            VMEM((max(n_x - 1, 1), 8, wide_y), F32),
            VMEM((max(n_y - 1, 1), 8, wide_z), F32),
            VMEM((max(n_z - 1, 1), 8, wide_own), F32),
            VMEM((max(n_x - 1, 1), 8, wide_y), F32),
            VMEM((max(n_y - 1, 1), 8, wide_z), F32),
            VMEM((max(n_z - 1, 1), 8, wide_own), F32),
            VMEM((8, wide_y), F32),
            VMEM((8, wide_z), F32),
            VMEM((3, 8, width), F32),
            VMEM((8, width), F32),
            VMEM((hops, 4, local), F32),
            DMA((8,)),
            DMA((1,)),
            DMA((4,)),
            DMA((4, heads)),
            DMA((1,)),
            DMA((1,)),
            DMA((HALVES,)),
            DMA((HALVES,)),
            DMA((1,)),
            DMA((heads,)),
            DMA((HALVES - 1,)),
            DMA((HALVES - 1,)),
            DMA((3,)),
            DMA((3,)),
            DMA((1,)),
            DMA((1,)),
            DMA((4,)),
            DMA((4,)),
            DMA((4,)),
            DMA((4,)),
            DMA((3,)),
            DMA((1,)),
        ],
        compiler_params=pltpu.CompilerParams(
            collective_id=0, has_side_effects=True, vmem_limit_bytes=44 << 20
        ),
    )(modulation, gains, condition, residual, query, key, value, residual_grad, mod_grad)


def results_kernel(factor, *refs):
    sources, sums_ref, targets, params_ref, sem = refs[:4], refs[4], refs[5:9], refs[9], refs[10]
    copies = [
        pltpu.make_async_copy(source, target, sem.at[i])
        for i, (source, target) in enumerate(zip(sources, targets))
    ]
    for copy in copies:
        copy.start()
    rows, own = params_ref.shape
    params_ref[...] = sums_ref[0:rows, 0:own] * factor
    for copy in copies:
        copy.wait()


def results(factor, own, parts):
    hbm = pl.BlockSpec(memory_space=pltpu.HBM)
    vmem = pl.BlockSpec(memory_space=VMEM)
    big = [jax.ShapeDtypeStruct(part.shape, part.dtype) for part in parts[:4]]
    return pl.pallas_call(
        functools.partial(results_kernel, factor),
        out_shape=(*big, jax.ShapeDtypeStruct((5, own), F32)),
        in_specs=[vmem] * 4 + [vmem],
        out_specs=(*([hbm] * 4), vmem),
        scratch_shapes=[DMA((4,))],
        compiler_params=pltpu.CompilerParams(vmem_limit_bytes=8 << 20),
    )(*parts)


def per_device(
    layout,
    residual,
    query_raw,
    key_raw,
    values,
    residual_grad,
    modulated_grad,
    condition,
    modulation,
    norm_gains,
):
    residual, query_raw, key_raw, values, residual_grad, modulated_grad = (
        pltpu.with_memory_space_constraint(x, pltpu.HBM)
        for x in (residual, query_raw, key_raw, values, residual_grad, modulated_grad)
    )
    condition, modulation, norm_gains = (
        pltpu.with_memory_space_constraint(x, pltpu.HBM)
        for x in (condition[0], modulation, norm_gains)
    )
    factor = (residual.shape[0] * lax.axis_size("seq") * lax.axis_size("dp")) ** (-0.5)
    return results(
        factor,
        modulation.shape[1],
        whole_block(
            layout,
            modulation,
            norm_gains,
            condition,
            residual,
            query_raw,
            key_raw,
            values,
            residual_grad,
            modulated_grad,
        ),
    )


def solution(mesh):
    layout = (8, 4, mesh.shape["dp"] // 32) if mesh.shape["dp"] >= 32 else (mesh.shape["dp"], 1, 1)
    rows = P(("seq", "dp"), None)
    columns = P(None, ("seq", "dp"))
    return jax.shard_map(
        functools.partial(per_device, layout),
        mesh=mesh,
        in_specs=(rows,) * 6 + (P("dp", None, None), columns, columns),
        out_specs=(rows,) * 4 + (columns,),
        check_vma=False,
    )
```
